256 devices in a mesh: nodes: 8 (over x, core), batch: 32 (over z, y).
Axes of the slice: x: 4, y: 4, z: 8, core: 2. Of those that a mesh axis runs over, the one named last changes fastest.
Arguments:
- leaves: float32 [16, 128, 4096], P('nodes', None, 'batch'), may hold values from -340 to 8
- prod_child: int32 [16, 2], replicated, may hold values from 0 to 15
- block_weight: float32 [1024, 128, 128], P('nodes'), may hold values from 0.0001 to 0.01
- block_child: int32 [8, 128], P('nodes'), may hold values from 0 to 15
- block_parent: int32 [8, 128], P('nodes'), may hold values from 0 to 3, as said below
- block_count: int32 [8], P('nodes'), may hold values from 32 to 128, as said below
- upper_flow: float32 [32, 128, 4096], P('nodes', None, 'batch'), may hold values from 0.1 to 1
Outputs:
- sum_values: float32 [32, 128, 4096], P('nodes', None, 'batch')
- leaf_flow: float32 [16, 128, 4096], P('nodes', None, 'batch')
- param_flow: float32 [1024, 128, 128], P(('nodes', 'batch'))
The draws below stay inside these ranges and needn't reach their ends.
Inputs may be any that keep to these rules, and one draw needn't show every extreme that they name: `block_parent`: every owner's first 4 slots name its sum groups 0 to 3 in order. `block_count`: some owner has all 128 slots live.
All inputs are finite; a program needn't handle non-finite values.
Results may differ from the reference program's by a relative error of at most 0.0003.
Values sent between devices are 32-bit elements; how exact they have to be, the bound alone decides.
No kernel may reach another device: no remote copies, remote signals or barrier semaphores. Data moves between devices by JAX's collectives and lax.ppermute only.
A program may use at most 128 MiB of HBM per device.

```python
import math
import jax
import jax.numpy as jnp
from jax import lax

G = 128
QD = 4
BPO = 128
NG = 16
PG = 16
QG = 32
NB = 1024
SAMPLES = 4096
N_NODES = 8


def draw_leaves(key, part):
    base_key = jax.random.fold_in(key, 11)
    shift_key = jax.random.fold_in(key, 12)
    base = jnp.clip(jax.random.normal(base_key, (NG, G, SAMPLES), jnp.float32), -6.0, 6.0)
    offset = jax.random.uniform(shift_key, (1, 1, SAMPLES), jnp.float32, -4.0, 0.0)
    return base - 2.0 + offset


def draw_block_parent(key, part):
    slots = jnp.arange(BPO, dtype=jnp.int32)[None, :]
    picked = jax.random.randint(jax.random.fold_in(key, 21), (N_NODES, BPO), 0, QD)
    return jnp.where(slots < QD, slots, picked).astype(jnp.int32)


def draw_block_count(key, part):
    counts = jax.random.randint(jax.random.fold_in(key, 31), (N_NODES,), BPO // 4, BPO + 1)
    fullest = jax.random.randint(jax.random.fold_in(key, 32), (), 0, N_NODES)
    return jnp.where(jnp.arange(N_NODES, dtype=jnp.int32) == fullest, BPO, counts).astype(jnp.int32)


def set_ends(entries, key, smallest, high):
    dims = entries.shape
    place = [jax.random.randint(jax.random.fold_in(key, axis), (), 0, dims[axis]) for axis in range(len(dims))]
    entries = entries.at[tuple(place)].set(smallest)
    longest = dims.index(max(dims))
    place[longest] = (place[longest] + 1) % dims[longest]
    return entries.at[tuple(place)].set(high)


def level_of(rng, shape, cuts, least, top_value):
    factor_of, own = 1.0, jax.random.fold_in(rng, 6)
    for axis_at, parts in cuts:
        steps = jnp.exp(jax.random.uniform(jax.random.fold_in(own, axis_at), (parts,), jnp.float32, least / len(cuts), top_value / len(cuts)))
        factor_of = factor_of * jnp.repeat(steps, shape[axis_at] // parts).reshape([-1 if axis == axis_at else 1 for axis in range(len(shape))])
    return factor_of


def setup_inputs(seed: int = 0) -> dict:
    arg_keys = jax.random.split(jax.random.key(seed), 8)
    leaves = draw_leaves(jax.random.fold_in(arg_keys[7], 71), 0)
    prod_child = set_ends(jax.random.randint(arg_keys[1], (PG, 2), 0, NG), jax.random.fold_in(arg_keys[1], 1), 0, NG - 1).astype(jnp.int32)
    block_weight = jnp.clip(jnp.exp(math.log(0.01) - 4.6051702 * jax.random.uniform(arg_keys[2], (NB, G, G), jnp.float32) ** level_of(arg_keys[2], (NB, G, G), ((0, 8),), -0.2, 0.2)), 0.0001, 0.01)
    block_child = set_ends(jax.random.randint(arg_keys[3], (N_NODES, BPO), 0, PG), jax.random.fold_in(arg_keys[3], 1), 0, PG - 1).astype(jnp.int32)
    block_parent = draw_block_parent(jax.random.fold_in(arg_keys[7], 71), 0)
    block_count = draw_block_count(jax.random.fold_in(arg_keys[7], 71), 0)
    upper_flow = jnp.clip(jnp.exp(math.log(1.0) - 2.3025851 * jax.random.uniform(arg_keys[6], (QG, G, SAMPLES), jnp.float32) ** level_of(arg_keys[6], (QG, G, SAMPLES), ((0, 8), (2, 32)), -0.2, 0.2)), 0.1, 1.0)
    return dict(leaves=leaves, prod_child=prod_child, block_weight=block_weight, block_child=block_child, block_parent=block_parent, block_count=block_count, upper_flow=upper_flow)


very_low = -1e30


def reference(leaves, prod_child, block_weight, block_child, block_parent, block_count, upper_flow):
    high = lax.Precision.HIGHEST
    products = leaves[prod_child[:, 0]] + leaves[prod_child[:, 1]]
    peak = jnp.max(products, axis=1)
    owners = block_child.shape[0]
    per_owner = block_child.shape[1]
    groups_each = upper_flow.shape[0] // owners
    child = block_child.reshape(-1)
    parent = (block_parent + (jnp.arange(owners, dtype=jnp.int32) * groups_each)[:, None]).reshape(-1)
    live = (jnp.arange(per_owner, dtype=jnp.int32)[None, :] < block_count[:, None]).reshape(-1)
    top = jax.ops.segment_max(jnp.where(live[:, None], peak[child], very_low), parent, num_segments=upper_flow.shape[0])

    def shifted_of(c, q, l):
        return jnp.exp(jnp.where(l, products[c] - top[q][None, :], very_low))

    def forward(total, item):
        c, q, l, w = item
        sh = shifted_of(c, q, l)
        return total.at[q].add(jnp.dot(w, sh, precision=high, preferred_element_type=jnp.float32)), None

    total = lax.scan(forward, jnp.zeros(upper_flow.shape, jnp.float32), (child, parent, live, block_weight))[0]
    sum_values = top[:, None, :] + jnp.log(total)
    factor = upper_flow / total

    def backward(flows, item):
        c, q, l, w = item
        sh = shifted_of(c, q, l)
        par = factor[q]
        back = jnp.dot(w.T, par, precision=high, preferred_element_type=jnp.float32)
        flows = flows.at[c].add(sh * back)
        weight_flow = w * jnp.dot(par, sh.T, precision=high, preferred_element_type=jnp.float32)
        return flows, weight_flow

    product_flow, param_flow = lax.scan(backward, jnp.zeros(products.shape, jnp.float32), (child, parent, live, block_weight))
    leaf_flow = jnp.zeros(leaves.shape, jnp.float32).at[prod_child[:, 0]].add(product_flow)
    leaf_flow = leaf_flow.at[prod_child[:, 1]].add(product_flow)
    return sum_values, leaf_flow, param_flow
```

```python
import functools

import jax
import jax.numpy as jnp
from jax import lax
from jax.experimental import pallas as pl
from jax.experimental.pallas import tpu as pltpu
from jax.sharding import PartitionSpec as P

very_low = -1e30
f32, bf16 = jnp.float32, jnp.bfloat16
CORES = 2
ROWS = 4
VMEM = pltpu.VMEM
SMEM = pltpu.SMEM


def parts(x):
    hi = x.astype(bf16)
    lo = (x - hi.astype(f32)).astype(bf16)
    return hi, lo


def quadrants(x):
    g = x.shape[0] // 2
    return (x[:g, :g] + x[:g, g:]) + (x[g:, :g] + x[g:, g:])


def node_at(dx, dc, nodes):
    me = lax.axis_index("nodes")
    x, core = me // CORES, me % CORES
    chips = nodes // CORES
    return ((x + dx) % chips) * CORES + (core + dc) % CORES


def hops(nodes):
    return [(dx, dc) for dx in range(nodes // CORES) for dc in range(CORES)]


def vmem_specs(n):
    return [pl.BlockSpec(memory_space=VMEM)] * n


def fold_kernel(qd, child, parent, count, w_ref, whl, thl, bias, acc):
    step = pl.program_id(0)
    each = w_ref.shape[0]
    g = w_ref.shape[1]
    pg = thl.shape[0]

    @pl.when(step == 0)
    def _():
        bias[...] = jnp.full(bias.shape, very_low, f32)

        def clear(c, carry):
            acc[c] = jnp.zeros(acc.shape[1:], f32)
            return carry

        lax.fori_loop(0, acc.shape[0], clear, 0)

    for t in range(each):
        b = step * each + t

        @pl.when(b < count[0])
        def _():
            c, q = child[0, b], parent[0, b]
            acc[c * qd + q] += w_ref[t]
            bias[pl.ds(q * pg + c, 1), :] = jnp.zeros((1, bias.shape[1]), f32)

    @pl.when(step == pl.num_programs(0) - 1)
    def _():
        def convert(c, carry):
            at = pl.ds(pl.multiple_of(c * g, g), g)
            for q in range(qd):
                x = acc[c * qd + q]
                hi, lo = parts(x)
                whl[q, 0:g, at] = hi
                whl[q, g : 2 * g, at] = lo
                hi, lo = parts(x.T)
                thl[c, 0:g, q * g : (q + 1) * g] = hi
                thl[c, g : 2 * g, q * g : (q + 1) * g] = lo
            return carry

        lax.fori_loop(0, pg, convert, 0)


def fold(block_child, block_parent, block_count, block_weight, pg, qd):
    blocks, g, _ = block_weight.shape
    each = 8
    return pl.pallas_call(
        functools.partial(fold_kernel, qd),
        out_shape=(
            jax.ShapeDtypeStruct((qd, 2 * g, pg * g), bf16),
            jax.ShapeDtypeStruct((pg, 2 * g, qd * g), bf16),
            jax.ShapeDtypeStruct((qd * pg, g), f32),
        ),
        grid_spec=pltpu.PrefetchScalarGridSpec(
            num_scalar_prefetch=3,
            grid=(blocks // each,),
            in_specs=[pl.BlockSpec((each, g, g), lambda i, *_: (i, 0, 0))],
            out_specs=(
                pl.BlockSpec((qd, 2 * g, pg * g), lambda i, *_: (0, 0, 0)),
                pl.BlockSpec((pg, 2 * g, qd * g), lambda i, *_: (0, 0, 0)),
                pl.BlockSpec((qd * pg, g), lambda i, *_: (0, 0)),
            ),
            scratch_shapes=[VMEM((pg * qd, g, g), f32)],
        ),
        cost_estimate=pl.CostEstimate(flops=20_000_000, bytes_accessed=16 << 20, transcendentals=0),
        name="fold",
    )(block_child, block_parent, block_count, block_weight)


def forward_kernel(nodes, prod_child, *refs):
    n = nodes
    got = refs[:n]
    whl, bias, up, sv, fx, e_ref, r_ref, pk_ref, lv, shl, peak = refs[n:]
    pg, g, s = e_ref.shape
    q = pl.program_id(0)

    @pl.when(q == 0)
    def _():
        for k, (dx, dc) in enumerate(hops(n)):
            src = node_at(-dx, -dc, n)
            each = got[k].shape[0]
            lv[pl.ds(src * each, each)] = got[k][...]

        def product(p, carry):
            x = lv[prod_child[p, 0]] + lv[prod_child[p, 1]]
            m = jnp.max(x, axis=0, keepdims=True)
            peak[pl.ds(p, 1), :] = m
            e_ref[p] = jnp.exp(x - m)
            return carry

        lax.fori_loop(0, pg, product, 0, unroll=2)
        pk_ref[...] = peak[...]

    biased = peak[...] + bias[...]
    top = jnp.max(biased, axis=0, keepdims=True)
    r_ref[...] = jnp.exp(biased - top)

    def scaled(c, carry):
        hi, lo = parts(e_ref[c] * r_ref[pl.ds(c, 1), :])
        at = pl.ds(pl.multiple_of(c * g, g), g)
        shl[at, 0:s] = hi
        shl[at, s : 2 * s] = lo
        return carry

    lax.fori_loop(0, pg, scaled, 0, unroll=2)
    total = quadrants(jnp.dot(whl[0], shl[...], preferred_element_type=f32))
    sv[0] = top + jnp.log(total)
    fx[0, 0:g] = up[0] / total
    fx[0, g:] = jnp.broadcast_to(top, (8, s))


def forward(prod_child, got, whl, bias, up):
    nodes = len(got)
    qd, g, s = up.shape
    pg = prod_child.shape[0]
    one = lambda *shape: pl.BlockSpec(shape, lambda q, *_: (q,) + (0,) * (len(shape) - 1))
    whole = lambda *shape: pl.BlockSpec(shape, lambda q, *_: (0,) * len(shape))
    return pl.pallas_call(
        functools.partial(forward_kernel, nodes),
        out_shape=(
            jax.ShapeDtypeStruct((qd, g, s), f32),
            jax.ShapeDtypeStruct((qd, g + 8, s), f32),
            jax.ShapeDtypeStruct((pg, g, s), f32),
            jax.ShapeDtypeStruct((qd * pg, s), f32),
            jax.ShapeDtypeStruct((pg, s), f32),
        ),
        grid_spec=pltpu.PrefetchScalarGridSpec(
            num_scalar_prefetch=1,
            grid=(qd,),
            in_specs=[whole(*got[0].shape)] * nodes
            + [one(1, 2 * g, pg * g), one(pg, g), one(1, g, s)],
            out_specs=(one(1, g, s), one(1, g + 8, s), whole(pg, g, s), one(pg, s), whole(pg, s)),
            scratch_shapes=[
                VMEM((got[0].shape[0] * nodes, g, s), f32),
                VMEM((pg * g, 2 * s), bf16),
                VMEM((pg, s), f32),
            ],
        ),
        cost_estimate=pl.CostEstimate(
            flops=2 * qd * 4 * g * s * pg * g, bytes_accessed=8 << 20, transcendentals=pg * g * s
        ),
        name="forward",
    )(prod_child, *got, whl, bias, up)


def backward_kernel(nodes, prod_child, thl, fx, r_ref, e_ref, *refs):
    outs, (lf, ghl) = refs[:nodes], refs[nodes:]
    c = pl.program_id(0)
    qd = fx.shape[0]
    g, s = e_ref.shape[1:]
    pg = pl.num_programs(0)

    @pl.when(c == 0)
    def _():
        lf[...] = jnp.zeros(lf.shape, f32)

    for q in range(qd):
        hi, lo = parts(fx[q, 0:g] * r_ref[pl.ds(q * pg + c, 1), :])
        ghl[q * g : (q + 1) * g, 0:s] = hi
        ghl[q * g : (q + 1) * g, s : 2 * s] = lo
    back = quadrants(jnp.dot(thl[0], ghl[...], preferred_element_type=f32))
    flow = back * e_ref[0]
    lf[prod_child[c, 0]] += flow
    lf[prod_child[c, 1]] += flow

    @pl.when(c == pg - 1)
    def _():
        for k, (dx, dc) in enumerate(hops(nodes)):
            each = outs[k].shape[0]
            outs[k][...] = lf[pl.ds(node_at(dx, dc, nodes) * each, each)]


def backward(prod_child, thl, fx, r, e, nodes, ng):
    pg, g, s = e.shape
    qd = fx.shape[0]
    whole = lambda *shape: pl.BlockSpec(shape, lambda q, *_: (0,) * len(shape))
    one = lambda *shape: pl.BlockSpec(shape, lambda q, *_: (q,) + (0,) * (len(shape) - 1))
    each = ng // nodes
    return pl.pallas_call(
        functools.partial(backward_kernel, nodes),
        out_shape=[jax.ShapeDtypeStruct((each, g, s), f32)] * nodes,
        grid_spec=pltpu.PrefetchScalarGridSpec(
            num_scalar_prefetch=1,
            grid=(pg,),
            in_specs=[
                one(1, 2 * g, qd * g),
                whole(*fx.shape),
                whole(*r.shape),
                one(1, g, s),
            ],
            out_specs=[whole(each, g, s)] * nodes,
            scratch_shapes=[VMEM((ng, g, s), f32), VMEM((qd * g, 2 * s), bf16)],
        ),
        cost_estimate=pl.CostEstimate(
            flops=2 * qd * 4 * g * s * pg * g, bytes_accessed=8 << 20, transcendentals=0
        ),
        name="backward",
    )(prod_child, thl, fx, r, e)


def spread_kernel(prod_child, offsets, e_own, pk_own, *refs):
    k = len(offsets)
    pieces, (ehl, pk, lv) = refs[: 2 * k], refs[2 * k :]
    pg, g, s = e_own.shape
    nodes = lv.shape[0] // 2
    sets = lv.shape[1]
    for k, (dx, dc) in enumerate(offsets):
        src = node_at(-dx, -dc, nodes)
        for j in range(2):
            lv[src * 2 + j] = pieces[2 * k + j][...]

    def product(p, carry):
        hi, lo = parts(e_own[p])
        ehl[p, 0:g, 0:s] = hi
        ehl[p, g : 2 * g, 0:s] = lo
        pk[0, pl.ds(p, 1), :] = pk_own[pl.ds(p, 1), :]
        a, b = prod_child[p, 0], prod_child[p, 1]
        for t in range(sets):
            x = lv[a, t] + lv[b, t]
            m = jnp.max(x, axis=0, keepdims=True)
            at = slice((t + 1) * s, (t + 2) * s)
            pk[t + 1, pl.ds(p, 1), :] = m
            hi, lo = parts(jnp.exp(x - m))
            ehl[p, 0:g, at] = hi
            ehl[p, g : 2 * g, at] = lo
        return carry

    lax.fori_loop(0, pg, product, 0)


def spread(prod_child, e, pk, pieces, offsets, nodes):
    pg, g, s = e.shape
    sets = pieces[0].shape[0]

    def kernel(pc, *refs):
        spread_kernel(pc, offsets, *refs)

    return pl.pallas_call(
        kernel,
        out_shape=(
            jax.ShapeDtypeStruct((pg, 2 * g, (sets + 1) * s), bf16),
            jax.ShapeDtypeStruct((sets + 1, pg, s), f32),
        ),
        in_specs=[pl.BlockSpec(memory_space=SMEM)] + vmem_specs(2 + len(pieces)),
        out_specs=tuple(vmem_specs(2)),
        scratch_shapes=[VMEM((nodes * 2, sets, g, s), f32)],
        cost_estimate=pl.CostEstimate(
            flops=10_000_000, bytes_accessed=10 << 20, transcendentals=pg * g * s * sets
        ),
        name="spread",
    )(prod_child, e, pk, *pieces)


def edges_kernel(dists, child, parent, count, ehl, pk, bias, *refs):
    rows = ROWS
    fxs, refs = refs[:rows], refs[rows:]
    outs, (fac, r, lhs) = refs[:-3], refs[-3:]
    qd, s = fxs[0].shape[0], fxs[0].shape[2]
    g = fxs[0].shape[1] - 8
    pg = pk.shape[1]
    batch = lax.axis_index("batch")
    z, y = batch // ROWS, batch % ROWS
    depth = lax.axis_size("batch") // ROWS
    for q in range(qd):
        for t in range(rows):
            at = slice(t * s, (t + 1) * s)
            fac[q, :, at] = fxs[t][q, 0:g]
            top = fxs[t][q, g : g + 1]
            r[t, q * pg : (q + 1) * pg, :] = jnp.exp(
                (pk[t] + bias[q * pg : (q + 1) * pg, :]) - top
            )
    half = outs[0].shape[0]
    keep = 2 * half
    for d, k0, out in zip(dists[0], dists[1], outs):
        base = ((z + d + depth) % depth * ROWS + y) * keep + k0

        def slot(k, carry, base=base, out=out):
            b = base + k

            @pl.when(b < count[0])
            def _():
                c, q = child[0, b], parent[0, b]
                for t in range(rows):
                    at = slice(t * s, (t + 1) * s)
                    hi, lo = parts(fac[q, :, at] * r[t, pl.ds(q * pg + c, 1), :])
                    lhs[0:g, at] = hi
                    lhs[g : 2 * g, at] = lo
                out[k] = quadrants(
                    lax.dot_general(
                        lhs[...], ehl[c], (((1,), (1,)), ((), ())), preferred_element_type=f32
                    )
                )

            @pl.when(b >= count[0])
            def _():
                out[k] = jnp.zeros((g, g), f32)

            return carry

        lax.fori_loop(0, half, slot, 0)


def edges(child, parent, count, ehl, pk, bias, fxs, ds, ks, half):
    g = ehl.shape[1] // 2
    pg, width = pk.shape[1], ehl.shape[2]
    qd = fxs[0].shape[0]

    def kernel(*refs):
        edges_kernel((ds, ks), *refs)

    return pl.pallas_call(
        kernel,
        out_shape=[jax.ShapeDtypeStruct((half, g, g), f32)] * len(ds),
        in_specs=[pl.BlockSpec(memory_space=SMEM)] * 3 + vmem_specs(3 + len(fxs)),
        out_specs=vmem_specs(len(ds)),
        scratch_shapes=[
            VMEM((qd, g, width), f32),
            VMEM((len(fxs), qd * pg, width // len(fxs)), f32),
            VMEM((2 * g, width), bf16),
        ],
        cost_estimate=pl.CostEstimate(
            flops=2 * len(ds) * half * 4 * g * g * width, bytes_accessed=8 << 20, transcendentals=0
        ),
        name="edges",
    )(child, parent, count, ehl, pk, bias, *fxs)


def body(leaves, prod_child, block_weight, block_child, block_parent, block_count, upper_flow):
    nodes = lax.axis_size("nodes")
    batch = lax.axis_size("batch")
    chips, depth = nodes // CORES, batch // ROWS
    ng = leaves.shape[0] * nodes
    pg = prod_child.shape[0]
    qd = upper_flow.shape[0]
    keep = block_weight.shape[0] // batch
    half = keep // 2

    def move(a, dx=0, dc=0):
        to = lambda n: ((n // CORES + dx) % chips) * CORES + (n % CORES + dc) % CORES
        return lax.ppermute(a, "nodes", [(n, to(n)) for n in range(nodes)])

    def shift(a, dz=0, dy=0):
        to = lambda b: ((b // ROWS + dz) % depth) * ROWS + (b % ROWS + dy) % ROWS
        return lax.ppermute(a, "batch", [(b, to(b)) for b in range(batch)])

    got = [leaves if (dx, dc) == (0, 0) else move(leaves, dx, dc) for dx, dc in hops(nodes)]
    row = [shift(leaves, dy=t) for t in range(1, ROWS)]
    own = [jnp.stack([a[j] for a in row]) for j in range(2)]
    plus = [move(a, 1) for a in own]
    minus = [move(a, -1) for a in own]
    far = [move(plus[0], 1), move(minus[1], -1)]
    same = [(0, own), (1, plus), (-1, minus), (2, far)]
    offsets, pieces = [], []
    for dx, pair in same:
        offsets += [(dx, 0), (dx, 1)]
        pieces += pair + [move(a, 0, 1) for a in pair]

    whl, thl, bias = fold(block_child, block_parent, block_count, block_weight, pg, qd)
    sum_values, fx, e, r, pk = forward(prod_child, got, whl, bias, upper_flow)
    fxs = [fx] + [shift(fx, dy=t) for t in range(1, ROWS)]
    flows = backward(prod_child, thl, fx, r, e, nodes, ng)
    back = [a if h == (0, 0) else move(a, *h) for h, a in zip(hops(nodes), flows)]
    leaf_flow = functools.reduce(jnp.add, back)

    ehl, pks = spread(prod_child, e, pk, pieces, offsets, nodes)
    ds, ks = [], []
    for d in range(depth // 2, -1, -1):
        for sign in (1, -1):
            for k in (0, half):
                if d == depth // 2 and (sign == 1) != (k == 0):
                    continue
                if d == 0 and sign == -1:
                    continue
                ds.append(sign * d)
                ks.append(k)
    part = dict(
        zip(zip(ds, ks), edges(block_child, block_parent, block_count, ehl, pks, bias, fxs, ds, ks, half))
    )
    wt = lax.dynamic_slice_in_dim(block_weight, lax.axis_index("batch") * keep, keep, 0)
    total = []
    for k in (0, half):
        send = {}
        for d in range(depth // 2, 0, -1):
            for sign in (1, -1):
                a = part.get((sign * d, k))
                if a is None:
                    continue
                if sign in send:
                    a = a + send[sign]
                send[sign] = shift(a, dz=sign)
        total.append(part[(0, k)] + send[1] + send[-1])
    param_flow = jnp.concatenate(total) * wt
    return sum_values, leaf_flow, param_flow


def solution(mesh):
    placed = (
        P("nodes", None, "batch"),
        P(),
        P("nodes", None, None),
        P("nodes", None),
        P("nodes", None),
        P("nodes"),
        P("nodes", None, "batch"),
    )
    return jax.shard_map(
        body,
        mesh=mesh,
        in_specs=placed,
        out_specs=(
            P("nodes", None, "batch"),
            P("nodes", None, "batch"),
            P(("nodes", "batch"), None, None),
        ),
        check_vma=False,
    )
```

```python
import functools

import jax
import jax.numpy as jnp
from jax import lax
from jax.experimental import pallas as pl
from jax.experimental.pallas import tpu as pltpu
from jax.sharding import PartitionSpec as P

very_low = -1e30
f32, bf16 = jnp.float32, jnp.bfloat16
CORES = 2
ROWS = 4
VMEM = pltpu.VMEM
SMEM = pltpu.SMEM


def parts(x):
    hi = x.astype(bf16)
    lo = (x - hi.astype(f32)).astype(bf16)
    return hi, lo


def quadrants(x):
    g = x.shape[0] // 2
    return (x[:g, :g] + x[:g, g:]) + (x[g:, :g] + x[g:, g:])


def node_at(dx, dc, nodes):
    me = lax.axis_index("nodes")
    x, core = me // CORES, me % CORES
    chips = nodes // CORES
    return ((x + dx) % chips) * CORES + (core + dc) % CORES


def hops(nodes):
    return [(dx, dc) for dx in range(nodes // CORES) for dc in range(CORES)]


def vmem_specs(n):
    return [pl.BlockSpec(memory_space=VMEM)] * n


def fold_kernel(child, parent, count, w_ref, acc, bias):
    step = pl.program_id(0)
    each = w_ref.shape[0]
    pg = acc.shape[1]

    @pl.when(step == 0)
    def _():
        bias[...] = jnp.full(bias.shape, very_low, f32)

        def clear(c, carry):
            for q in range(acc.shape[0]):
                acc[q, c] = jnp.zeros(acc.shape[2:], f32)
            return carry

        lax.fori_loop(0, pg, clear, 0)

    def add(t, carry):
        b = step * each + t

        @pl.when(b < count[0])
        def _():
            c, q = child[0, b], parent[0, b]
            acc[q, c] += w_ref[t]
            bias[pl.ds(q * pg + c, 1), :] = jnp.zeros((1, bias.shape[1]), f32)

        return carry

    lax.fori_loop(0, each, add, 0)


def fold(block_child, block_parent, block_count, block_weight, pg, qd):
    blocks, g, _ = block_weight.shape
    each = 16
    return pl.pallas_call(
        fold_kernel,
        out_shape=(
            jax.ShapeDtypeStruct((qd, pg, g, g), f32),
            jax.ShapeDtypeStruct((qd * pg, g), f32),
        ),
        grid_spec=pltpu.PrefetchScalarGridSpec(
            num_scalar_prefetch=3,
            grid=(blocks // each,),
            in_specs=[pl.BlockSpec((each, g, g), lambda i, *_: (i, 0, 0))],
            out_specs=(
                pl.BlockSpec((qd, pg, g, g), lambda i, *_: (0, 0, 0, 0)),
                pl.BlockSpec((qd * pg, g), lambda i, *_: (0, 0)),
            ),
        ),
        compiler_params=pltpu.CompilerParams(vmem_limit_bytes=16 << 20),
        cost_estimate=pl.CostEstimate(flops=20_000_000, bytes_accessed=16 << 20, transcendentals=0),
        name="fold",
    )(block_child, block_parent, block_count, block_weight)


def forward_kernel(nodes, prod_child, *refs):
    n = nodes
    got = refs[:n]
    w_ref, bias, up, sv, fx, e_ref, r_ref, pk_ref, lv, whl, shl, peak = refs[n:]
    pg, g, s = e_ref.shape
    q = pl.program_id(0)

    @pl.when(q == 0)
    def _():
        for k, (dx, dc) in enumerate(hops(n)):
            src = node_at(-dx, -dc, n)
            each = got[k].shape[0]
            lv[pl.ds(src * each, each)] = got[k][...]

        def product(p, carry):
            x = lv[prod_child[p, 0]] + lv[prod_child[p, 1]]
            m = jnp.max(x, axis=0, keepdims=True)
            peak[pl.ds(p, 1), :] = m
            e_ref[p] = jnp.exp(x - m)
            return carry

        lax.fori_loop(0, pg, product, 0, unroll=2)
        pk_ref[...] = peak[...]

    biased = peak[...] + bias[...]
    top = jnp.max(biased, axis=0, keepdims=True)
    r_ref[...] = jnp.exp(biased - top)

    def scaled(c, carry):
        at = pl.ds(pl.multiple_of(c * g, g), g)
        hi, lo = parts(w_ref[0, c])
        whl[0:g, at] = hi
        whl[g : 2 * g, at] = lo
        hi, lo = parts(e_ref[c] * r_ref[pl.ds(c, 1), :])
        shl[at, 0:s] = hi
        shl[at, s : 2 * s] = lo
        return carry

    lax.fori_loop(0, pg, scaled, 0, unroll=2)
    total = quadrants(jnp.dot(whl[...], shl[...], preferred_element_type=f32))
    sv[0] = top + jnp.log(total)
    fx[0, 0:g] = up[0] / total
    fx[0, g:] = jnp.broadcast_to(top, (8, s))


def forward(prod_child, got, w, bias, up):
    nodes = len(got)
    qd, g, s = up.shape
    pg = prod_child.shape[0]
    one = lambda *shape: pl.BlockSpec(shape, lambda q, *_: (q,) + (0,) * (len(shape) - 1))
    whole = lambda *shape: pl.BlockSpec(shape, lambda q, *_: (0,) * len(shape))
    return pl.pallas_call(
        functools.partial(forward_kernel, nodes),
        out_shape=(
            jax.ShapeDtypeStruct((qd, g, s), f32),
            jax.ShapeDtypeStruct((qd, g + 8, s), f32),
            jax.ShapeDtypeStruct((pg, g, s), f32),
            jax.ShapeDtypeStruct((qd * pg, s), f32),
            jax.ShapeDtypeStruct((pg, s), f32),
        ),
        grid_spec=pltpu.PrefetchScalarGridSpec(
            num_scalar_prefetch=1,
            grid=(qd,),
            in_specs=[whole(*got[0].shape)] * nodes
            + [one(1, pg, g, g), one(pg, g), one(1, g, s)],
            out_specs=(one(1, g, s), one(1, g + 8, s), whole(pg, g, s), one(pg, s), whole(pg, s)),
            scratch_shapes=[
                VMEM((got[0].shape[0] * nodes, g, s), f32),
                VMEM((2 * g, pg * g), bf16),
                VMEM((pg * g, 2 * s), bf16),
                VMEM((pg, s), f32),
            ],
        ),
        compiler_params=pltpu.CompilerParams(vmem_limit_bytes=20 << 20),
        cost_estimate=pl.CostEstimate(
            flops=2 * qd * 4 * g * s * pg * g, bytes_accessed=8 << 20, transcendentals=pg * g * s
        ),
        name="forward",
    )(prod_child, *got, w, bias, up)


def backward_kernel(nodes, prod_child, w_ref, fx, r_ref, e_ref, token, *refs):
    chips = nodes // CORES
    keep, give, (lf, thl, ghl) = refs[:chips], refs[chips], refs[chips + 1 :]
    step = pl.program_id(0)
    qd = fx.shape[0]
    each, g, s = e_ref.shape
    pg = each * pl.num_programs(0)

    @pl.when(step == 0)
    def _():
        lf[...] = jnp.zeros(lf.shape, f32)

    for t in range(each):
        c = step * each + t
        for q in range(qd):
            at = slice(q * g, (q + 1) * g)
            hi, lo = parts(w_ref[q, t].T)
            thl[t, 0:g, at] = hi
            thl[t, g : 2 * g, at] = lo
            hi, lo = parts(fx[q, 0:g] * r_ref[pl.ds(q * pg + c, 1), :])
            ghl[t, at, 0:s] = hi
            ghl[t, at, s : 2 * s] = lo
    for t in range(each):
        c = step * each + t
        back = quadrants(jnp.dot(thl[t], ghl[t], preferred_element_type=f32))
        flow = back * e_ref[t]
        lf[prod_child[c, 0]] += flow
        lf[prod_child[c, 1]] += flow

    @pl.when(step == pl.num_programs(0) - 1)
    def _():
        for dx in range(chips):
            k = keep[0].shape[0]
            keep[dx][...] = lf[pl.ds(node_at(dx, 0, nodes) * k, k)]
            give[dx * k : (dx + 1) * k] = lf[pl.ds(node_at(dx, 1, nodes) * k, k)]


def backward(prod_child, w, fx, r, e, token, nodes, ng):
    pg, g, s = e.shape
    qd = fx.shape[0]
    chips = nodes // CORES
    each = 4
    whole = lambda *shape: pl.BlockSpec(shape, lambda q, *_: (0,) * len(shape))
    one = lambda *shape: pl.BlockSpec(shape, lambda q, *_: (q,) + (0,) * (len(shape) - 1))
    k = ng // nodes
    return pl.pallas_call(
        functools.partial(backward_kernel, nodes),
        out_shape=[jax.ShapeDtypeStruct((k, g, s), f32)] * chips
        + [jax.ShapeDtypeStruct((k * chips, g, s), f32)],
        grid_spec=pltpu.PrefetchScalarGridSpec(
            num_scalar_prefetch=1,
            grid=(pg // each,),
            in_specs=[
                pl.BlockSpec((qd, each, g, g), lambda i, *_: (0, i, 0, 0)),
                whole(*fx.shape),
                whole(*r.shape),
                one(each, g, s),
                pl.BlockSpec(memory_space=pl.ANY),
            ],
            out_specs=[whole(k, g, s)] * chips + [whole(k * chips, g, s)],
            scratch_shapes=[
                VMEM((ng, g, s), f32),
                VMEM((each, 2 * g, qd * g), bf16),
                VMEM((each, qd * g, 2 * s), bf16),
            ],
        ),
        compiler_params=pltpu.CompilerParams(vmem_limit_bytes=20 << 20),
        cost_estimate=pl.CostEstimate(
            flops=2 * qd * 4 * g * s * pg * g, bytes_accessed=8 << 20, transcendentals=0
        ),
        name="backward",
    )(prod_child, w, fx, r, e, token)


def pack_kernel(*refs):
    for t, a in enumerate(refs[:-1]):
        refs[-1][t] = a[...]


def pack(arrays):
    return pl.pallas_call(
        pack_kernel,
        out_shape=jax.ShapeDtypeStruct((len(arrays),) + arrays[0].shape, f32),
        in_specs=vmem_specs(len(arrays)),
        out_specs=vmem_specs(1)[0],
        compiler_params=pltpu.CompilerParams(vmem_limit_bytes=4 << 20),
        cost_estimate=pl.CostEstimate(flops=0, bytes_accessed=1 << 20, transcendentals=0),
        name="pack",
    )(*arrays)


def spread_kernel(offsets, prod_child, e_own, pk_own, *refs):
    pieces, (ehl, pk) = refs[: len(offsets)], refs[len(offsets) : -1]
    lv = refs[-1]
    pg, g, s = e_own.shape
    sets, each = pieces[0].shape[:2]
    nodes = lv.shape[1] // each
    for (dx, dc), piece in zip(offsets, pieces):
        src = node_at(-dx, -dc, nodes)
        for t in range(sets):
            lv[t, pl.ds(src * each, each)] = piece[t]

    def product(p, carry):
        hi, lo = parts(e_own[p])
        ehl[p, 0:g, 0:s] = hi
        ehl[p, g : 2 * g, 0:s] = lo
        pk[0, pl.ds(p, 1), :] = pk_own[pl.ds(p, 1), :]
        a, b = prod_child[p, 0], prod_child[p, 1]
        for t in range(sets):
            x = lv[t, a] + lv[t, b]
            m = jnp.max(x, axis=0, keepdims=True)
            at = slice((t + 1) * s, (t + 2) * s)
            pk[t + 1, pl.ds(p, 1), :] = m
            hi, lo = parts(jnp.exp(x - m))
            ehl[p, 0:g, at] = hi
            ehl[p, g : 2 * g, at] = lo
        return carry

    lax.fori_loop(0, pg, product, 0)


def spread(prod_child, e, pk, pieces, offsets, nodes):
    pg, g, s = e.shape
    sets, each = pieces[0].shape[:2]

    def kernel(*refs):
        spread_kernel(offsets, *refs)

    return pl.pallas_call(
        kernel,
        out_shape=(
            jax.ShapeDtypeStruct((pg, 2 * g, (sets + 1) * s), bf16),
            jax.ShapeDtypeStruct((sets + 1, pg, s), f32),
        ),
        in_specs=[pl.BlockSpec(memory_space=SMEM)] + vmem_specs(2 + len(pieces)),
        out_specs=tuple(vmem_specs(2)),
        scratch_shapes=[VMEM((sets, nodes * each, g, s), f32)],
        compiler_params=pltpu.CompilerParams(vmem_limit_bytes=20 << 20),
        cost_estimate=pl.CostEstimate(
            flops=10_000_000, bytes_accessed=10 << 20, transcendentals=pg * g * s * sets
        ),
        name="spread",
    )(prod_child, e, pk, *pieces)


def edges_kernel(plan, child, parent, count, ehl, pk, bias, *refs):
    rows = ROWS
    fxs, refs = refs[:rows], refs[rows:]
    token, outs, (r, lhs) = refs[0], refs[1:-2], refs[-2:]
    qd, s = fxs[0].shape[0], fxs[0].shape[2]
    g = fxs[0].shape[1] - 8
    pg = pk.shape[1]
    batch = lax.axis_index("batch")
    z, y = batch // ROWS, batch % ROWS
    depth = lax.axis_size("batch") // ROWS
    for q in range(qd):
        for t in range(rows):
            top = fxs[t][q, g : g + 1]
            here = slice(q * pg, (q + 1) * pg)
            r[t, here, :] = jnp.exp((pk[t] + bias[here, :]) - top)
    for (d, k0, n, keep), out in zip(plan, outs):
        base = ((z + d + depth) % depth * ROWS + y) * keep + k0
        for k in range(n):
            b = base + k
            c, q = child[0, b], parent[0, b]
            live = (b < count[0]).astype(f32)
            for t in range(rows):
                at = slice(t * s, (t + 1) * s)
                hi, lo = parts(fxs[t][q, 0:g] * (r[t, pl.ds(q * pg + c, 1), :] * live))
                lhs[k, 0:g, at] = hi
                lhs[k, g : 2 * g, at] = lo
        for k in range(n):
            c = child[0, base + k]
            out[k] = quadrants(
                lax.dot_general(
                    lhs[k], ehl[c], (((1,), (1,)), ((), ())), preferred_element_type=f32
                )
            )


def edges(child, parent, count, ehl, pk, bias, fxs, token, plan):
    g = ehl.shape[1] // 2
    pg, width = pk.shape[1], ehl.shape[2]
    qd = fxs[0].shape[0]
    slots = sum(n for _, _, n, _ in plan)

    def kernel(*refs):
        edges_kernel(plan, *refs)

    return pl.pallas_call(
        kernel,
        out_shape=[jax.ShapeDtypeStruct((n, g, g), f32) for _, _, n, _ in plan],
        in_specs=[pl.BlockSpec(memory_space=SMEM)] * 3
        + vmem_specs(3 + len(fxs))
        + [pl.BlockSpec(memory_space=pl.ANY)],
        out_specs=vmem_specs(len(plan)),
        scratch_shapes=[
            VMEM((len(fxs), qd * pg, width // len(fxs)), f32),
            VMEM((max(n for _, _, n, _ in plan), 2 * g, width), bf16),
        ],
        compiler_params=pltpu.CompilerParams(vmem_limit_bytes=20 << 20),
        cost_estimate=pl.CostEstimate(
            flops=2 * slots * 4 * g * g * width, bytes_accessed=6 << 20, transcendentals=0
        ),
        name="edges",
    )(child, parent, count, ehl, pk, bias, *fxs, token)


def join_kernel(at, a_ref, b_ref, c_ref, token, out):
    n = c_ref.shape[0]
    out[...] = a_ref[...] + b_ref[...]
    out[at : at + n] += c_ref[...]


def join(a, b, c, token, at):
    return pl.pallas_call(
        functools.partial(join_kernel, at),
        out_shape=jax.ShapeDtypeStruct(a.shape, f32),
        in_specs=vmem_specs(3) + [pl.BlockSpec(memory_space=pl.ANY)],
        out_specs=vmem_specs(1)[0],
        compiler_params=pltpu.CompilerParams(vmem_limit_bytes=4 << 20),
        cost_estimate=pl.CostEstimate(flops=200_000, bytes_accessed=1 << 20, transcendentals=0),
        name="join",
    )(a, b, c, token)


def body(leaves, prod_child, block_weight, block_child, block_parent, block_count, upper_flow):
    nodes = lax.axis_size("nodes")
    batch = lax.axis_size("batch")
    chips, depth = nodes // CORES, batch // ROWS
    ng = leaves.shape[0] * nodes
    pg = prod_child.shape[0]
    qd = upper_flow.shape[0]
    keep = block_weight.shape[0] // batch
    half = keep // 2
    far = depth // 2

    def move(a, dx=0, dc=0):
        to = lambda n: ((n // CORES + dx) % chips) * CORES + (n % CORES + dc) % CORES
        return lax.ppermute(a, "nodes", [(n, to(n)) for n in range(nodes)])

    def shift(a, dz=0, dy=0):
        to = lambda b: ((b // ROWS + dz) % depth) * ROWS + (b % ROWS + dy) % ROWS
        return lax.ppermute(a, "batch", [(b, to(b)) for b in range(batch)])

    def gather(a):
        out = []
        for dx in range(chips):
            got = move(a, dx) if dx else a
            out += [got, move(got, 0, 1)]
        return out

    row = [shift(leaves, dy=t) for t in range(1, ROWS)]
    got = gather(leaves)
    pieces = gather(pack(row))

    w, bias = fold(block_child, block_parent, block_count, block_weight, pg, qd)
    sum_values, fx, e, r, pk = forward(prod_child, got, w, bias, upper_flow)
    fxs = [fx] + [shift(fx, dy=t) for t in range(1, ROWS)]
    ehl, pks = spread(prod_child, e, pk, pieces, hops(nodes), nodes)

    def part(token, *plan):
        return edges(block_child, block_parent, block_count, ehl, pks, bias, fxs, token, plan)

    e4p, e4m, e3p, e3m = part(
        pks, (far, 0, half, keep), (-far, half, half, keep), (3, 0, keep, keep), (-3, 0, keep, keep)
    )
    r4p, r4m = shift(e4p, dz=2), shift(e4m, dz=-2)
    r3p, r3m = shift(e3p, dz=1), shift(e3m, dz=-1)
    e1p, e1m = part(e3m, (1, 0, keep, keep), (-1, 0, keep, keep))
    r1p, r1m = shift(e1p, dz=1), shift(e1m, dz=-1)
    e2p, e2m, e0 = part(e1m, (2, 0, keep, keep), (-2, 0, keep, keep), (0, 0, keep, keep))
    *mine, give = backward(prod_child, w, fx, r, e, e0, nodes, ng)
    r2p = shift(join(e2p, r3p, r4p, give, 0), dz=2)
    r2m = shift(join(e2m, r3m, r4m, give, half), dz=-2)
    given = move(give, 0, 1)
    k = leaves.shape[0]
    flows = [a + given[dx * k : (dx + 1) * k] for dx, a in enumerate(mine)]
    leaf_flow = functools.reduce(
        jnp.add, [flows[0]] + [move(flows[dx], dx) for dx in range(1, chips)]
    )
    wt = lax.dynamic_slice_in_dim(block_weight, lax.axis_index("batch") * keep, keep, 0)
    param_flow = wt * ((e0 + r1p + r1m) + (r2p + r2m))
    return sum_values, leaf_flow, param_flow


def solution(mesh):
    placed = (
        P("nodes", None, "batch"),
        P(),
        P("nodes", None, None),
        P("nodes", None),
        P("nodes", None),
        P("nodes"),
        P("nodes", None, "batch"),
    )
    return jax.shard_map(
        body,
        mesh=mesh,
        in_specs=placed,
        out_specs=(
            P("nodes", None, "batch"),
            P("nodes", None, "batch"),
            P(("nodes", "batch"), None, None),
        ),
        check_vma=False,
    )
```

```python
import functools

import jax
import jax.numpy as jnp
from jax import lax
from jax.experimental import pallas as pl
from jax.experimental.pallas import tpu as pltpu
from jax.sharding import PartitionSpec as P


very_low = -1e30
f32, bf16 = jnp.float32, jnp.bfloat16
CORES = 2
ROWS = 4
VMEM = pltpu.VMEM
SMEM = pltpu.SMEM


def parts(x):
    hi = x.astype(bf16)
    lo = (x - hi.astype(f32)).astype(bf16)
    return hi, lo


def quadrants(x):
    g = x.shape[0] // 2
    return (x[:g, :g] + x[:g, g:]) + (x[g:, :g] + x[g:, g:])


def node_at(dx, dc, nodes):
    me = lax.axis_index("nodes")
    x, core = me // CORES, me % CORES
    chips = nodes // CORES
    return ((x + dx) % chips) * CORES + (core + dc) % CORES


def hops(nodes):
    return [(dx, dc) for dx in range(nodes // CORES) for dc in range(CORES)]


def vmem_specs(n):
    return [pl.BlockSpec(memory_space=VMEM)] * n


def fold_kernel(child, parent, count, w_ref, acc, bias):
    step = pl.program_id(0)
    each = w_ref.shape[0]
    pg = acc.shape[1]

    @pl.when(step == 0)
    def _():
        bias[...] = jnp.full(bias.shape, very_low, f32)

        def clear(c, carry):
            for q in range(acc.shape[0]):
                acc[q, c] = jnp.zeros(acc.shape[2:], f32)
            return carry

        lax.fori_loop(0, pg, clear, 0)

    def add(t, carry):
        b = step * each + t

        @pl.when(b < count[0])
        def _():
            c, q = child[0, b], parent[0, b]
            acc[q, c] += w_ref[t]
            bias[pl.ds(q * pg + c, 1), :] = jnp.zeros((1, bias.shape[1]), f32)

        return carry

    lax.fori_loop(0, each, add, 0)


def fold(block_child, block_parent, block_count, block_weight, pg, qd):
    blocks, g, _ = block_weight.shape
    each = 16
    return pl.pallas_call(
        fold_kernel,
        out_shape=(
            jax.ShapeDtypeStruct((qd, pg, g, g), f32),
            jax.ShapeDtypeStruct((qd * pg, g), f32),
        ),
        grid_spec=pltpu.PrefetchScalarGridSpec(
            num_scalar_prefetch=3,
            grid=(blocks // each,),
            in_specs=[pl.BlockSpec((each, g, g), lambda i, *_: (i, 0, 0))],
            out_specs=(
                pl.BlockSpec((qd, pg, g, g), lambda i, *_: (0, 0, 0, 0)),
                pl.BlockSpec((qd * pg, g), lambda i, *_: (0, 0)),
            ),
        ),
        compiler_params=pltpu.CompilerParams(vmem_limit_bytes=46 << 20),
        cost_estimate=pl.CostEstimate(flops=20_000_000, bytes_accessed=16 << 20, transcendentals=0),
        name="fold",
    )(block_child, block_parent, block_count, block_weight)


def forward_kernel(nodes, prod_child, *refs):
    n = nodes
    got = refs[:n]
    w_ref, bias, up, sv, fx, e_ref, r_ref, pk_ref, lv, whl, shl, peak = refs[n:]
    pg, g, s = e_ref.shape
    q = pl.program_id(0)

    @pl.when(q == 0)
    def _():
        for k, (dx, dc) in enumerate(hops(n)):
            src = node_at(-dx, -dc, n)
            each = got[k].shape[0]
            lv[pl.ds(src * each, each)] = got[k][...]

        def product(p, carry):
            x = lv[prod_child[0, p]] + lv[prod_child[1, p]]
            m = jnp.max(x, axis=0, keepdims=True)
            peak[pl.ds(p, 1), :] = m
            e_ref[p] = jnp.exp(x - m)
            return carry

        lax.fori_loop(0, pg, product, 0, unroll=2)
        pk_ref[...] = peak[...]

    biased = peak[...] + bias[...]
    top = jnp.max(biased, axis=0, keepdims=True)
    r_ref[...] = jnp.exp(biased - top)

    def scaled(c, carry):
        at = pl.ds(pl.multiple_of(c * g, g), g)
        hi, lo = parts(w_ref[0, c])
        whl[0:g, at] = hi
        whl[g : 2 * g, at] = lo
        hi, lo = parts(e_ref[c] * r_ref[pl.ds(c, 1), :])
        shl[at, 0:s] = hi
        shl[at, s : 2 * s] = lo
        return carry

    lax.fori_loop(0, pg, scaled, 0, unroll=2)
    total = quadrants(jnp.dot(whl[...], shl[...], preferred_element_type=f32))
    sv[0] = top + jnp.log(total)
    fx[0, 0:g] = up[0] / total
    fx[0, g:] = jnp.broadcast_to(top, (8, s))


def forward(prod_child, got, w, bias, up):
    nodes = len(got)
    qd, g, s = up.shape
    pg = prod_child.shape[1]
    one = lambda *shape: pl.BlockSpec(shape, lambda q, *_: (q,) + (0,) * (len(shape) - 1))
    whole = lambda *shape: pl.BlockSpec(shape, lambda q, *_: (0,) * len(shape))
    return pl.pallas_call(
        functools.partial(forward_kernel, nodes),
        out_shape=(
            jax.ShapeDtypeStruct((qd, g, s), f32),
            jax.ShapeDtypeStruct((qd, g + 8, s), f32),
            jax.ShapeDtypeStruct((pg, g, s), f32),
            jax.ShapeDtypeStruct((qd * pg, s), f32),
            jax.ShapeDtypeStruct((pg, s), f32),
        ),
        grid_spec=pltpu.PrefetchScalarGridSpec(
            num_scalar_prefetch=1,
            grid=(qd,),
            in_specs=[whole(*got[0].shape)] * nodes
            + [one(1, pg, g, g), one(pg, g), one(1, g, s)],
            out_specs=(one(1, g, s), one(1, g + 8, s), whole(pg, g, s), one(pg, s), whole(pg, s)),
            scratch_shapes=[
                VMEM((got[0].shape[0] * nodes, g, s), f32),
                VMEM((2 * g, pg * g), bf16),
                VMEM((pg * g, 2 * s), bf16),
                VMEM((pg, s), f32),
            ],
        ),
        compiler_params=pltpu.CompilerParams(vmem_limit_bytes=20 << 20),
        cost_estimate=pl.CostEstimate(
            flops=2 * qd * 4 * g * s * pg * g, bytes_accessed=8 << 20, transcendentals=pg * g * s
        ),
        name="forward",
    )(prod_child, *got, w, bias, up)


def backward_kernel(nodes, prod_child, w_ref, fx, r_ref, e_ref, token, *refs):
    chips = nodes // CORES
    keep, give, (lf, thl, ghl) = refs[:chips], refs[chips], refs[chips + 1 :]
    step = pl.program_id(0)
    qd = fx.shape[0]
    each, g, s = e_ref.shape
    pg = each * pl.num_programs(0)

    @pl.when(step == 0)
    def _():
        lf[...] = jnp.zeros(lf.shape, f32)

    for t in range(each):
        c = step * each + t
        for q in range(qd):
            at = slice(q * g, (q + 1) * g)
            hi, lo = parts(w_ref[q, t].T)
            thl[t, 0:g, at] = hi
            thl[t, g : 2 * g, at] = lo
            hi, lo = parts(fx[q, 0:g] * r_ref[pl.ds(q * pg + c, 1), :])
            ghl[t, at, 0:s] = hi
            ghl[t, at, s : 2 * s] = lo
    for t in range(each):
        c = step * each + t
        back = quadrants(jnp.dot(thl[t], ghl[t], preferred_element_type=f32))
        flow = back * e_ref[t]
        lf[prod_child[0, c]] += flow
        lf[prod_child[1, c]] += flow

    @pl.when(step == pl.num_programs(0) - 1)
    def _():
        for dx in range(chips):
            k = keep[0].shape[0]
            keep[dx][...] = lf[pl.ds(node_at(dx, 0, nodes) * k, k)]
            give[dx * k : (dx + 1) * k] = lf[pl.ds(node_at(dx, 1, nodes) * k, k)]


def backward(prod_child, w, fx, r, e, token, nodes, ng):
    pg, g, s = e.shape
    qd = fx.shape[0]
    chips = nodes // CORES
    each = 4
    whole = lambda *shape: pl.BlockSpec(shape, lambda q, *_: (0,) * len(shape))
    one = lambda *shape: pl.BlockSpec(shape, lambda q, *_: (q,) + (0,) * (len(shape) - 1))
    k = ng // nodes
    return pl.pallas_call(
        functools.partial(backward_kernel, nodes),
        out_shape=[jax.ShapeDtypeStruct((k, g, s), f32)] * chips
        + [jax.ShapeDtypeStruct((k * chips, g, s), f32)],
        grid_spec=pltpu.PrefetchScalarGridSpec(
            num_scalar_prefetch=1,
            grid=(pg // each,),
            in_specs=[
                pl.BlockSpec((qd, each, g, g), lambda i, *_: (0, i, 0, 0)),
                whole(*fx.shape),
                whole(*r.shape),
                one(each, g, s),
                pl.BlockSpec(memory_space=pl.ANY),
            ],
            out_specs=[whole(k, g, s)] * chips + [whole(k * chips, g, s)],
            scratch_shapes=[
                VMEM((ng, g, s), f32),
                VMEM((each, 2 * g, qd * g), bf16),
                VMEM((each, qd * g, 2 * s), bf16),
            ],
        ),
        compiler_params=pltpu.CompilerParams(vmem_limit_bytes=20 << 20),
        cost_estimate=pl.CostEstimate(
            flops=2 * qd * 4 * g * s * pg * g, bytes_accessed=8 << 20, transcendentals=0
        ),
        name="backward",
    )(prod_child, w, fx, r, e, token)


def pack_kernel(*refs):
    for t, a in enumerate(refs[:-1]):
        refs[-1][t] = a[...]


def pack(arrays):
    return pl.pallas_call(
        pack_kernel,
        out_shape=jax.ShapeDtypeStruct((len(arrays),) + arrays[0].shape, f32),
        in_specs=vmem_specs(len(arrays)),
        out_specs=vmem_specs(1)[0],
        compiler_params=pltpu.CompilerParams(vmem_limit_bytes=4 << 20),
        cost_estimate=pl.CostEstimate(flops=0, bytes_accessed=1 << 20, transcendentals=0),
        name="pack",
    )(*arrays)


def spread_kernel(offsets, prod_child, e_own, pk_own, *refs):
    pieces, (ehl, pk) = refs[: len(offsets)], refs[len(offsets) : -1]
    lv = refs[-1]
    pg, g, s = e_own.shape
    sets, each = pieces[0].shape[:2]
    nodes = lv.shape[1] // each
    for (dx, dc), piece in zip(offsets, pieces):
        src = node_at(-dx, -dc, nodes)
        for t in range(sets):
            lv[t, pl.ds(src * each, each)] = piece[t]

    def product(p, carry):
        hi, lo = parts(e_own[p])
        ehl[p, 0:g, 0:s] = hi
        ehl[p, g : 2 * g, 0:s] = lo
        pk[0, pl.ds(p, 1), :] = pk_own[pl.ds(p, 1), :]
        a, b = prod_child[0, p], prod_child[1, p]
        for t in range(sets):
            x = lv[t, a] + lv[t, b]
            m = jnp.max(x, axis=0, keepdims=True)
            at = slice((t + 1) * s, (t + 2) * s)
            pk[t + 1, pl.ds(p, 1), :] = m
            hi, lo = parts(jnp.exp(x - m))
            ehl[p, 0:g, at] = hi
            ehl[p, g : 2 * g, at] = lo
        return carry

    lax.fori_loop(0, pg, product, 0)


def spread(prod_child, e, pk, pieces, offsets, nodes):
    pg, g, s = e.shape
    sets, each = pieces[0].shape[:2]

    def kernel(*refs):
        spread_kernel(offsets, *refs)

    return pl.pallas_call(
        kernel,
        out_shape=(
            jax.ShapeDtypeStruct((pg, 2 * g, (sets + 1) * s), bf16),
            jax.ShapeDtypeStruct((sets + 1, pg, s), f32),
        ),
        in_specs=[pl.BlockSpec(memory_space=SMEM)] + vmem_specs(2 + len(pieces)),
        out_specs=tuple(vmem_specs(2)),
        scratch_shapes=[VMEM((sets, nodes * each, g, s), f32)],
        compiler_params=pltpu.CompilerParams(vmem_limit_bytes=20 << 20),
        cost_estimate=pl.CostEstimate(
            flops=10_000_000, bytes_accessed=10 << 20, transcendentals=pg * g * s * sets
        ),
        name="spread",
    )(prod_child, e, pk, *pieces)


def edges_kernel(plan, child, parent, count, ehl, pk, bias, *refs):
    rows = ROWS
    fxs, refs = refs[:rows], refs[rows:]
    outs, (r, lhs) = refs[1:-2], refs[-2:]
    qd, s = fxs[0].shape[0], fxs[0].shape[2]
    g = fxs[0].shape[1] - 8
    pg = pk.shape[1]
    batch = lax.axis_index("batch")
    z, y = batch // ROWS, batch % ROWS
    depth = lax.axis_size("batch") // ROWS
    for q in range(qd):
        for t in range(rows):
            top = fxs[t][q, g : g + 1]
            here = slice(q * pg, (q + 1) * pg)
            r[t, here, :] = jnp.exp((pk[t] + bias[here, :]) - top)
    for (d, k0, n, keep), out in zip(plan, outs):
        base = ((z + d + depth) % depth * ROWS + y) * keep + k0
        for k in range(n):
            b = base + k
            c, q = child[0, b], parent[0, b]
            live = (b < count[0]).astype(f32)
            for t in range(rows):
                at = slice(t * s, (t + 1) * s)
                hi, lo = parts(fxs[t][q, 0:g] * (r[t, pl.ds(q * pg + c, 1), :] * live))
                lhs[k, 0:g, at] = hi
                lhs[k, g : 2 * g, at] = lo
        for k in range(n):
            c = child[0, base + k]
            out[k] = quadrants(
                lax.dot_general(
                    lhs[k], ehl[c], (((1,), (1,)), ((), ())), preferred_element_type=f32
                )
            )


def edges(child, parent, count, ehl, pk, bias, fxs, token, plan):
    g = ehl.shape[1] // 2
    pg, width = pk.shape[1], ehl.shape[2]
    qd = fxs[0].shape[0]
    slots = sum(n for _, _, n, _ in plan)

    def kernel(*refs):
        edges_kernel(plan, *refs)

    return pl.pallas_call(
        kernel,
        out_shape=[jax.ShapeDtypeStruct((n, g, g), f32) for _, _, n, _ in plan],
        in_specs=[pl.BlockSpec(memory_space=SMEM)] * 3
        + vmem_specs(3 + len(fxs))
        + [pl.BlockSpec(memory_space=pl.ANY)],
        out_specs=vmem_specs(len(plan)),
        scratch_shapes=[
            VMEM((len(fxs), qd * pg, width // len(fxs)), f32),
            VMEM((max(n for _, _, n, _ in plan), 2 * g, width), bf16),
        ],
        compiler_params=pltpu.CompilerParams(vmem_limit_bytes=20 << 20),
        cost_estimate=pl.CostEstimate(
            flops=2 * slots * 4 * g * g * width, bytes_accessed=6 << 20, transcendentals=0
        ),
        name="edges",
    )(child, parent, count, ehl, pk, bias, *fxs, token)


def join_kernel(at, a_ref, b_ref, c_ref, token, out):
    n = c_ref.shape[0]
    out[...] = a_ref[...] + b_ref[...]
    out[at : at + n] += c_ref[...]


def join(a, b, c, token, at):
    return pl.pallas_call(
        functools.partial(join_kernel, at),
        out_shape=jax.ShapeDtypeStruct(a.shape, f32),
        in_specs=vmem_specs(3) + [pl.BlockSpec(memory_space=pl.ANY)],
        out_specs=vmem_specs(1)[0],
        compiler_params=pltpu.CompilerParams(vmem_limit_bytes=4 << 20),
        cost_estimate=pl.CostEstimate(flops=200_000, bytes_accessed=1 << 20, transcendentals=0),
        name="join",
    )(a, b, c, token)


def body(leaves, prod_child, block_weight, block_child, block_parent, block_count, upper_flow):
    prod_child = prod_child.T
    nodes = lax.axis_size("nodes")
    batch = lax.axis_size("batch")
    chips, depth = nodes // CORES, batch // ROWS
    ng = leaves.shape[0] * nodes
    pg = prod_child.shape[1]
    qd = upper_flow.shape[0]
    keep = block_weight.shape[0] // batch
    half = keep // 2
    far = depth // 2

    def move(a, dx=0, dc=0):
        to = lambda n: ((n // CORES + dx) % chips) * CORES + (n % CORES + dc) % CORES
        return lax.ppermute(a, "nodes", [(n, to(n)) for n in range(nodes)])

    def shift(a, dz=0, dy=0):
        to = lambda b: ((b // ROWS + dz) % depth) * ROWS + (b % ROWS + dy) % ROWS
        return lax.ppermute(a, "batch", [(b, to(b)) for b in range(batch)])

    def gather(a):
        out = []
        for dx in range(chips):
            got = move(a, dx) if dx else a
            out += [got, move(got, 0, 1)]
        return out

    got = gather(leaves)
    row = [shift(leaves, dy=t) for t in range(1, ROWS)]
    packed = pack(row)
    pieces = gather(packed)

    w, bias = fold(block_child, block_parent, block_count, block_weight, pg, qd)
    sum_values, fx, e, r, pk = forward(prod_child, got, w, bias, upper_flow)
    fxs = [fx] + [shift(fx, dy=t) for t in range(1, ROWS)]
    ehl, pks = spread(prod_child, e, pk, pieces, hops(nodes), nodes)

    def part(token, *plan):
        return edges(
            block_child, block_parent, block_count, ehl, pks, bias, fxs, token, plan
        )

    e4p, e4m, e3p, e3m = part(
        pks, (far, 0, half, keep), (-far, half, half, keep), (3, 0, keep, keep), (-3, 0, keep, keep)
    )
    r4p, r4m = shift(e4p, dz=2), shift(e4m, dz=-2)
    r3p, r3m = shift(e3p, dz=1), shift(e3m, dz=-1)
    e1p, e1m = part(e3m, (1, 0, keep, keep), (-1, 0, keep, keep))
    r1p, r1m = shift(e1p, dz=1), shift(e1m, dz=-1)
    e2p, e2m, e0 = part(e1m, (2, 0, keep, keep), (-2, 0, keep, keep), (0, 0, keep, keep))
    *mine, give = backward(prod_child, w, fx, r, e, e0, nodes, ng)
    c2p = join(e2p, r3p, r4p, give, 0)
    c2m = join(e2m, r3m, r4m, give, half)
    r2p, r2m = shift(c2p, dz=2), shift(c2m, dz=-2)
    given = move(give, 0, 1)
    k = leaves.shape[0]
    flows = [a + given[dx * k : (dx + 1) * k] for dx, a in enumerate(mine)]
    leaf_flow = functools.reduce(
        jnp.add, [flows[0]] + [move(flows[dx], dx) for dx in range(1, chips)]
    )
    wt = lax.dynamic_slice_in_dim(block_weight, lax.axis_index("batch") * keep, keep, 0)
    param_flow = wt * ((e0 + r1p + r1m) + (r2p + r2m))
    return sum_values, leaf_flow, param_flow


def solution(mesh):
    placed = (
        P("nodes", None, "batch"),
        P(),
        P("nodes", None, None),
        P("nodes", None),
        P("nodes", None),
        P("nodes"),
        P("nodes", None, "batch"),
    )
    return jax.shard_map(
        body,
        mesh=mesh,
        in_specs=placed,
        out_specs=(
            P("nodes", None, "batch"),
            P("nodes", None, "batch"),
            P(("nodes", "batch"), None, None),
        ),
        check_vma=False,
    )
```

```python
import functools

import jax
import jax.numpy as jnp
from jax import lax
from jax.experimental import pallas as pl
from jax.experimental.pallas import tpu as pltpu
from jax.sharding import PartitionSpec as P


very_low = -1e30
f32, bf16 = jnp.float32, jnp.bfloat16
CORES = 2
ROWS = 4
VMEM = pltpu.VMEM
SMEM = pltpu.SMEM


def parts(x):
    hi = x.astype(bf16)
    lo = (x - hi.astype(f32)).astype(bf16)
    return hi, lo


def quadrants(x):
    g = x.shape[0] // 2
    return (x[:g, :g] + x[:g, g:]) + (x[g:, :g] + x[g:, g:])


def node_at(dx, dc, nodes):
    me = lax.axis_index("nodes")
    x, core = me // CORES, me % CORES
    chips = nodes // CORES
    return ((x + dx) % chips) * CORES + (core + dc) % CORES


def hops(nodes):
    return [(dx, dc) for dx in range(nodes // CORES) for dc in range(CORES)]


def vmem_specs(n):
    return [pl.BlockSpec(memory_space=VMEM)] * n


def fold_kernel(child, parent, count, w_ref, acc, bias):
    step = pl.program_id(0)
    each = w_ref.shape[0]
    pg = acc.shape[1]

    @pl.when(step == 0)
    def _():
        bias[...] = jnp.full(bias.shape, very_low, f32)

        def clear(c, carry):
            for q in range(acc.shape[0]):
                acc[q, c] = jnp.zeros(acc.shape[2:], f32)
            return carry

        lax.fori_loop(0, pg, clear, 0)

    def add(t, carry):
        b = step * each + t

        @pl.when(b < count[0])
        def _():
            c, q = child[0, b], parent[0, b]
            acc[q, c] += w_ref[t]
            bias[pl.ds(q * pg + c, 1), :] = jnp.zeros((1, bias.shape[1]), f32)

        return carry

    lax.fori_loop(0, each, add, 0)


def fold(block_child, block_parent, block_count, block_weight, pg, qd):
    blocks, g, _ = block_weight.shape
    each = 16
    return pl.pallas_call(
        fold_kernel,
        out_shape=(
            jax.ShapeDtypeStruct((qd, pg, g, g), f32),
            jax.ShapeDtypeStruct((qd * pg, g), f32),
        ),
        grid_spec=pltpu.PrefetchScalarGridSpec(
            num_scalar_prefetch=3,
            grid=(blocks // each,),
            in_specs=[pl.BlockSpec((each, g, g), lambda i, *_: (i, 0, 0))],
            out_specs=(
                pl.BlockSpec((qd, pg, g, g), lambda i, *_: (0, 0, 0, 0)),
                pl.BlockSpec((qd * pg, g), lambda i, *_: (0, 0)),
            ),
        ),
        compiler_params=pltpu.CompilerParams(vmem_limit_bytes=46 << 20),
        cost_estimate=pl.CostEstimate(flops=20_000_000, bytes_accessed=16 << 20, transcendentals=0),
        name="fold",
    )(block_child, block_parent, block_count, block_weight)


def forward_kernel(nodes, prod_child, *refs):
    n = nodes
    got = refs[:n]
    w_ref, bias, up, sv, fx, e_ref, r_ref, pk_ref, lv, whl, shl, peak = refs[n:]
    pg, g, s = e_ref.shape
    q = pl.program_id(0)

    @pl.when(q == 0)
    def _():
        for k, (dx, dc) in enumerate(hops(n)):
            src = node_at(-dx, -dc, n)
            each = got[k].shape[0]
            lv[pl.ds(src * each, each)] = got[k][...]

        def product(p, carry):
            x = lv[prod_child[0, p]] + lv[prod_child[1, p]]
            m = jnp.max(x, axis=0, keepdims=True)
            peak[pl.ds(p, 1), :] = m
            e_ref[p] = jnp.exp(x - m)
            return carry

        lax.fori_loop(0, pg, product, 0, unroll=2)
        pk_ref[...] = peak[...]

    biased = peak[...] + bias[...]
    top = jnp.max(biased, axis=0, keepdims=True)
    r_ref[...] = jnp.exp(biased - top)

    def scaled(c, carry):
        at = pl.ds(pl.multiple_of(c * g, g), g)
        hi, lo = parts(w_ref[0, c])
        whl[0:g, at] = hi
        whl[g : 2 * g, at] = lo
        hi, lo = parts(e_ref[c] * r_ref[pl.ds(c, 1), :])
        shl[at, 0:s] = hi
        shl[at, s : 2 * s] = lo
        return carry

    lax.fori_loop(0, pg, scaled, 0, unroll=2)
    total = quadrants(jnp.dot(whl[...], shl[...], preferred_element_type=f32))
    sv[0] = top + jnp.log(total)
    fx[0, 0:g] = up[0] / total
    fx[0, g:] = jnp.broadcast_to(top, (8, s))


def forward(prod_child, got, w, bias, up):
    nodes = len(got)
    qd, g, s = up.shape
    pg = prod_child.shape[1]
    one = lambda *shape: pl.BlockSpec(shape, lambda q, *_: (q,) + (0,) * (len(shape) - 1))
    whole = lambda *shape: pl.BlockSpec(shape, lambda q, *_: (0,) * len(shape))
    return pl.pallas_call(
        functools.partial(forward_kernel, nodes),
        out_shape=(
            jax.ShapeDtypeStruct((qd, g, s), f32),
            jax.ShapeDtypeStruct((qd, g + 8, s), f32),
            jax.ShapeDtypeStruct((pg, g, s), f32),
            jax.ShapeDtypeStruct((qd * pg, s), f32),
            jax.ShapeDtypeStruct((pg, s), f32),
        ),
        grid_spec=pltpu.PrefetchScalarGridSpec(
            num_scalar_prefetch=1,
            grid=(qd,),
            in_specs=[whole(*got[0].shape)] * nodes
            + [one(1, pg, g, g), one(pg, g), one(1, g, s)],
            out_specs=(one(1, g, s), one(1, g + 8, s), whole(pg, g, s), one(pg, s), whole(pg, s)),
            scratch_shapes=[
                VMEM((got[0].shape[0] * nodes, g, s), f32),
                VMEM((2 * g, pg * g), bf16),
                VMEM((pg * g, 2 * s), bf16),
                VMEM((pg, s), f32),
            ],
        ),
        compiler_params=pltpu.CompilerParams(vmem_limit_bytes=20 << 20),
        cost_estimate=pl.CostEstimate(
            flops=2 * qd * 4 * g * s * pg * g, bytes_accessed=8 << 20, transcendentals=pg * g * s
        ),
        name="forward",
    )(prod_child, *got, w, bias, up)


def backward_kernel(nodes, prod_child, w_ref, fx, r_ref, e_ref, token, *refs):
    chips = nodes // CORES
    keep, give, (lf, thl, ghl) = refs[:chips], refs[chips], refs[chips + 1 :]
    step = pl.program_id(0)
    qd = fx.shape[0]
    each, g, s = e_ref.shape
    pg = each * pl.num_programs(0)

    @pl.when(step == 0)
    def _():
        lf[...] = jnp.zeros(lf.shape, f32)

    for t in range(each):
        c = step * each + t
        for q in range(qd):
            at = slice(q * g, (q + 1) * g)
            hi, lo = parts(w_ref[q, t].T)
            thl[t, 0:g, at] = hi
            thl[t, g : 2 * g, at] = lo
            hi, lo = parts(fx[q, 0:g] * r_ref[pl.ds(q * pg + c, 1), :])
            ghl[t, at, 0:s] = hi
            ghl[t, at, s : 2 * s] = lo
    for t in range(each):
        c = step * each + t
        back = quadrants(jnp.dot(thl[t], ghl[t], preferred_element_type=f32))
        flow = back * e_ref[t]
        lf[prod_child[0, c]] += flow
        lf[prod_child[1, c]] += flow

    @pl.when(step == pl.num_programs(0) - 1)
    def _():
        for dx in range(chips):
            k = keep[0].shape[0]
            keep[dx][...] = lf[pl.ds(node_at(dx, 0, nodes) * k, k)]
            give[dx * k : (dx + 1) * k] = lf[pl.ds(node_at(dx, 1, nodes) * k, k)]


def backward(prod_child, w, fx, r, e, token, nodes, ng):
    pg, g, s = e.shape
    qd = fx.shape[0]
    chips = nodes // CORES
    each = 4
    whole = lambda *shape: pl.BlockSpec(shape, lambda q, *_: (0,) * len(shape))
    one = lambda *shape: pl.BlockSpec(shape, lambda q, *_: (q,) + (0,) * (len(shape) - 1))
    k = ng // nodes
    return pl.pallas_call(
        functools.partial(backward_kernel, nodes),
        out_shape=[jax.ShapeDtypeStruct((k, g, s), f32)] * chips
        + [jax.ShapeDtypeStruct((k * chips, g, s), f32)],
        grid_spec=pltpu.PrefetchScalarGridSpec(
            num_scalar_prefetch=1,
            grid=(pg // each,),
            in_specs=[
                pl.BlockSpec((qd, each, g, g), lambda i, *_: (0, i, 0, 0)),
                whole(*fx.shape),
                whole(*r.shape),
                one(each, g, s),
                pl.BlockSpec(memory_space=pl.ANY),
            ],
            out_specs=[whole(k, g, s)] * chips + [whole(k * chips, g, s)],
            scratch_shapes=[
                VMEM((ng, g, s), f32),
                VMEM((each, 2 * g, qd * g), bf16),
                VMEM((each, qd * g, 2 * s), bf16),
            ],
        ),
        compiler_params=pltpu.CompilerParams(vmem_limit_bytes=20 << 20),
        cost_estimate=pl.CostEstimate(
            flops=2 * qd * 4 * g * s * pg * g, bytes_accessed=8 << 20, transcendentals=0
        ),
        name="backward",
    )(prod_child, w, fx, r, e, token)


def pack_kernel(*refs):
    at = 0
    for a in refs[:-1]:
        n = a.shape[0]
        refs[-1][at : at + n] = a[...]
        at += n


def pack(arrays):
    n = sum(a.shape[0] for a in arrays)
    return pl.pallas_call(
        pack_kernel,
        out_shape=jax.ShapeDtypeStruct((n,) + arrays[0].shape[1:], f32),
        in_specs=vmem_specs(len(arrays)),
        out_specs=vmem_specs(1)[0],
        compiler_params=pltpu.CompilerParams(vmem_limit_bytes=4 << 20),
        cost_estimate=pl.CostEstimate(flops=0, bytes_accessed=1 << 20, transcendentals=0),
        name="pack",
    )(*arrays)


def spread_kernel(offsets, prod_child, e_own, pk_own, *refs):
    pieces, (ehl, pk) = refs[: len(offsets)], refs[len(offsets) : -1]
    lv = refs[-1]
    pg, g, s = e_own.shape
    sets = lv.shape[0]
    each = pieces[0].shape[0] // sets
    nodes = lv.shape[1] // each
    for (dx, dc), piece in zip(offsets, pieces):
        src = node_at(-dx, -dc, nodes)
        for t in range(sets):
            lv[t, pl.ds(src * each, each)] = piece[t * each : (t + 1) * each]

    def product(p, carry):
        hi, lo = parts(e_own[p])
        ehl[p, 0:g, 0:s] = hi
        ehl[p, g : 2 * g, 0:s] = lo
        pk[0, pl.ds(p, 1), :] = pk_own[pl.ds(p, 1), :]
        a, b = prod_child[0, p], prod_child[1, p]
        for t in range(sets):
            x = lv[t, a] + lv[t, b]
            m = jnp.max(x, axis=0, keepdims=True)
            at = slice((t + 1) * s, (t + 2) * s)
            pk[t + 1, pl.ds(p, 1), :] = m
            hi, lo = parts(jnp.exp(x - m))
            ehl[p, 0:g, at] = hi
            ehl[p, g : 2 * g, at] = lo
        return carry

    lax.fori_loop(0, pg, product, 0)


def spread(prod_child, e, pk, pieces, offsets, nodes):
    pg, g, s = e.shape
    sets = ROWS - 1
    each = pieces[0].shape[0] // sets

    def kernel(*refs):
        spread_kernel(offsets, *refs)

    return pl.pallas_call(
        kernel,
        out_shape=(
            jax.ShapeDtypeStruct((pg, 2 * g, (sets + 1) * s), bf16),
            jax.ShapeDtypeStruct((sets + 1, pg, s), f32),
        ),
        in_specs=[pl.BlockSpec(memory_space=SMEM)] + vmem_specs(2 + len(pieces)),
        out_specs=tuple(vmem_specs(2)),
        scratch_shapes=[VMEM((sets, nodes * each, g, s), f32)],
        compiler_params=pltpu.CompilerParams(vmem_limit_bytes=20 << 20),
        cost_estimate=pl.CostEstimate(
            flops=10_000_000, bytes_accessed=10 << 20, transcendentals=pg * g * s * sets
        ),
        name="spread",
    )(prod_child, e, pk, *pieces)


def edges_kernel(plan, child, parent, count, ehl, pk, bias, *refs):
    rows = ROWS
    fxs, refs = refs[:rows], refs[rows:]
    outs, (r, lhs) = refs[1:-2], refs[-2:]
    qd, s = fxs[0].shape[0], fxs[0].shape[2]
    g = fxs[0].shape[1] - 8
    pg = pk.shape[1]
    batch = lax.axis_index("batch")
    z, y = batch // ROWS, batch % ROWS
    depth = lax.axis_size("batch") // ROWS
    for q in range(qd):
        for t in range(rows):
            top = fxs[t][q, g : g + 1]
            here = slice(q * pg, (q + 1) * pg)
            r[t, here, :] = jnp.exp((pk[t] + bias[here, :]) - top)
    for (d, k0, n, keep), out in zip(plan, outs):
        base = ((z + d + depth) % depth * ROWS + y) * keep + k0
        for k in range(n):
            b = base + k
            c, q = child[0, b], parent[0, b]
            live = (b < count[0]).astype(f32)
            for t in range(rows):
                at = slice(t * s, (t + 1) * s)
                hi, lo = parts(fxs[t][q, 0:g] * (r[t, pl.ds(q * pg + c, 1), :] * live))
                lhs[k, 0:g, at] = hi
                lhs[k, g : 2 * g, at] = lo
        for k in range(n):
            c = child[0, base + k]
            out[k] = quadrants(
                lax.dot_general(
                    lhs[k], ehl[c], (((1,), (1,)), ((), ())), preferred_element_type=f32
                )
            )


def edges(child, parent, count, ehl, pk, bias, fxs, token, plan):
    g = ehl.shape[1] // 2
    pg, width = pk.shape[1], ehl.shape[2]
    qd = fxs[0].shape[0]
    slots = sum(n for _, _, n, _ in plan)

    def kernel(*refs):
        edges_kernel(plan, *refs)

    return pl.pallas_call(
        kernel,
        out_shape=[jax.ShapeDtypeStruct((n, g, g), f32) for _, _, n, _ in plan],
        in_specs=[pl.BlockSpec(memory_space=SMEM)] * 3
        + vmem_specs(3 + len(fxs))
        + [pl.BlockSpec(memory_space=pl.ANY)],
        out_specs=vmem_specs(len(plan)),
        scratch_shapes=[
            VMEM((len(fxs), qd * pg, width // len(fxs)), f32),
            VMEM((max(n for _, _, n, _ in plan), 2 * g, width), bf16),
        ],
        compiler_params=pltpu.CompilerParams(vmem_limit_bytes=20 << 20),
        cost_estimate=pl.CostEstimate(
            flops=2 * slots * 4 * g * g * width, bytes_accessed=6 << 20, transcendentals=0
        ),
        name="edges",
    )(child, parent, count, ehl, pk, bias, *fxs, token)


def join_kernel(ap, am, bp, bm, c_ref, outp, outm):
    first = (lax.axis_index("nodes") % CORES == 0).astype(f32)
    outp[...] = (ap[...] + bp[...]) + c_ref[...] * first
    outm[...] = (am[...] + bm[...]) + c_ref[...] * (1.0 - first)


def join(ap, am, bp, bm, c):
    return pl.pallas_call(
        join_kernel,
        out_shape=[jax.ShapeDtypeStruct(ap.shape, f32)] * 2,
        in_specs=vmem_specs(5),
        out_specs=vmem_specs(2),
        compiler_params=pltpu.CompilerParams(vmem_limit_bytes=4 << 20),
        cost_estimate=pl.CostEstimate(flops=400_000, bytes_accessed=2 << 20, transcendentals=0),
        name="join",
    )(ap, am, bp, bm, c)


def body(leaves, prod_child, block_weight, block_child, block_parent, block_count, upper_flow):
    prod_child = prod_child.T
    nodes = lax.axis_size("nodes")
    batch = lax.axis_size("batch")
    chips, depth = nodes // CORES, batch // ROWS
    ng = leaves.shape[0] * nodes
    pg = prod_child.shape[1]
    qd = upper_flow.shape[0]
    keep = block_weight.shape[0] // batch
    far = depth // 2

    def move(a, dx=0, dc=0):
        to = lambda n: ((n // CORES + dx) % chips) * CORES + (n % CORES + dc) % CORES
        return lax.ppermute(a, "nodes", [(n, to(n)) for n in range(nodes)])

    def shift(a, dz):
        to = lambda b: ((b // ROWS + dz) % depth) * ROWS + b % ROWS
        return lax.ppermute(a, "batch", [(b, to(b)) for b in range(batch)])

    def swap(a, mask):
        return lax.ppermute(a, "batch", [(b, b ^ mask) for b in range(batch)])

    def shift_by_core(a, dz):
        pairs = []
        for n in range(nodes):
            for b in range(batch):
                z = (b // ROWS + (dz if n % CORES == 0 else -dz)) % depth
                pairs.append((n * batch + b, n * batch + z * ROWS + b % ROWS))
        return lax.ppermute(a, ("nodes", "batch"), pairs)

    def gather(a):
        out = []
        for dx in range(chips):
            got = move(a, dx) if dx else a
            out += [got, move(got, 0, 1)]
        return out

    got = gather(leaves)
    one = swap(leaves, 1)
    pair = pack([leaves, one])
    two = swap(pair, 3)
    packed = pack([one, two])
    pieces = gather(packed)

    w, bias = fold(block_child, block_parent, block_count, block_weight, pg, qd)
    sum_values, fx, e, r, pk = forward(prod_child, got, w, bias, upper_flow)
    fxs = [fx] + [swap(fx, t) for t in (1, 3, 2)]
    *mine, give = backward(prod_child, w, fx, r, e, pk, nodes, ng)
    given = move(give, 0, 1)
    k = leaves.shape[0]
    flows = [a + given[dx * k : (dx + 1) * k] for dx, a in enumerate(mine)]
    ehl, pks = spread(prod_child, e, pk, pieces, hops(nodes), nodes)

    def part(token, *ds):
        plan = [(d, 0, keep, keep) for d in ds]
        return edges(
            block_child, block_parent, block_count, ehl, pks, bias, fxs, token, plan
        )

    (e4,) = part(pks, far)
    r4 = shift_by_core(e4, 2)
    e3p, e3m = part(e4, 3, -3)
    r3p, r3m = shift(e3p, 1), shift(e3m, -1)
    e1p, e1m, e0 = part(e3m, 1, -1, 0)
    r1p, r1m = shift(e1p, 1), shift(e1m, -1)
    e2p, e2m = part(e1m, 2, -2)
    c2p, c2m = join(e2p, e2m, r3p, r3m, r4)
    r2p, r2m = shift(c2p, 2), shift(c2m, -2)
    leaf_flow = functools.reduce(
        jnp.add, [flows[0]] + [move(flows[dx], dx) for dx in range(1, chips)]
    )
    wt = lax.dynamic_slice_in_dim(block_weight, lax.axis_index("batch") * keep, keep, 0)
    param_flow = wt * ((e0 + r1p + r1m) + (r2p + r2m))
    return sum_values, leaf_flow, param_flow


def solution(mesh):
    placed = (
        P("nodes", None, "batch"),
        P(),
        P("nodes", None, None),
        P("nodes", None),
        P("nodes", None),
        P("nodes"),
        P("nodes", None, "batch"),
    )
    return jax.shard_map(
        body,
        mesh=mesh,
        in_specs=placed,
        out_specs=(
            P("nodes", None, "batch"),
            P("nodes", None, "batch"),
            P(("nodes", "batch"), None, None),
        ),
        check_vma=False,
    )
```

```python
import functools

import jax
import jax.numpy as jnp
from jax import lax
from jax.experimental import pallas as pl
from jax.experimental.pallas import tpu as pltpu
from jax.sharding import PartitionSpec as P


very_low = -1e30
f32, bf16 = jnp.float32, jnp.bfloat16
CORES = 2
ROWS = 4
VMEM = pltpu.VMEM
SMEM = pltpu.SMEM


def parts(x):
    hi = x.astype(bf16)
    lo = (x - hi.astype(f32)).astype(bf16)
    return hi, lo


def quadrants(x):
    g = x.shape[0] // 2
    return (x[:g, :g] + x[:g, g:]) + (x[g:, :g] + x[g:, g:])


def node_at(dx, dc, nodes):
    me = lax.axis_index("nodes")
    x, core = me // CORES, me % CORES
    chips = nodes // CORES
    return ((x + dx) % chips) * CORES + (core + dc) % CORES


def hops(nodes):
    return [(dx, dc) for dx in range(nodes // CORES) for dc in range(CORES)]


def vmem_specs(n):
    return [pl.BlockSpec(memory_space=VMEM)] * n


def fold_kernel(each, count, slots_any, w_hbm, acc, bias, w, slots, sems, sem):
    pg = acc.shape[1]
    steps = w.shape[0] // each
    index = pltpu.make_async_copy(slots_any, slots, sem)
    index.start()
    copies = []
    for j in range(steps):
        at = pl.ds(j * each, each)
        copies.append(pltpu.make_async_copy(w_hbm.at[at], w.at[at], sems.at[j]))
        copies[j].start()

    bias[...] = jnp.full(bias.shape, very_low, f32)

    def clear(c, carry):
        for q in range(acc.shape[0]):
            acc[q, c] = jnp.zeros(acc.shape[2:], f32)
        return carry

    lax.fori_loop(0, pg, clear, 0)
    index.wait()
    for j in range(steps):
        copies[j].wait()

        def add(t, carry, j=j):
            b = j * each + t
            c, q = slots[0, b], slots[1, b]
            live = b < count[0]
            acc[q, c] += w[b] * live.astype(f32)
            row = pl.ds(q * pg + c, 1)
            bias[row, :] = jnp.where(live, 0.0, bias[row, :])
            return carry

        lax.fori_loop(0, each, add, 0, unroll=4)


def fold(slots, block_count, block_weight, pg, qd):
    blocks, g, _ = block_weight.shape
    each = 16
    return pl.pallas_call(
        functools.partial(fold_kernel, each),
        out_shape=(
            jax.ShapeDtypeStruct((qd, pg, g, g), f32),
            jax.ShapeDtypeStruct((qd * pg, g), f32),
        ),
        in_specs=[
            pl.BlockSpec(memory_space=SMEM),
            pl.BlockSpec(memory_space=pl.ANY),
            pl.BlockSpec(memory_space=pltpu.HBM),
        ],
        out_specs=tuple(vmem_specs(2)),
        scratch_shapes=[
            VMEM((blocks, g, g), f32),
            SMEM(slots.shape, jnp.int32),
            pltpu.SemaphoreType.DMA((blocks // each,)),
            pltpu.SemaphoreType.DMA,
        ],
        compiler_params=pltpu.CompilerParams(vmem_limit_bytes=46 << 20),
        cost_estimate=pl.CostEstimate(flops=20_000_000, bytes_accessed=16 << 20, transcendentals=0),
        name="fold",
    )(block_count, slots, block_weight)


def forward_kernel(nodes, prod_child, *refs):
    n = nodes
    got = refs[:n]
    w_ref, bias, up, sv, fx, e_ref, r_ref, pk, lv, whl, shl = refs[n:]
    pg, g, s = e_ref.shape
    for k, (dx, dc) in enumerate(hops(n)):
        src = node_at(-dx, -dc, n)
        each = got[k].shape[0]
        lv[pl.ds(src * each, each)] = got[k][...]

    def product(p, carry):
        x = lv[prod_child[0, p]] + lv[prod_child[1, p]]
        m = jnp.max(x, axis=0, keepdims=True)
        pk[pl.ds(p, 1), :] = m
        e_ref[p] = jnp.exp(x - m)
        return carry

    lax.fori_loop(0, pg, product, 0, unroll=2)
    for q in range(up.shape[0]):
        biased = pk[...] + bias[q * pg : (q + 1) * pg]
        top = jnp.max(biased, axis=0, keepdims=True)
        r_ref[q * pg : (q + 1) * pg] = jnp.exp(biased - top)

        def scaled(c, carry, q=q):
            at = pl.ds(pl.multiple_of(c * g, g), g)
            hi, lo = parts(w_ref[q, c])
            whl[q % 2, 0:g, at] = hi
            whl[q % 2, g : 2 * g, at] = lo
            hi, lo = parts(e_ref[c] * r_ref[pl.ds(q * pg + c, 1), :])
            shl[q % 2, at, 0:s] = hi
            shl[q % 2, at, s : 2 * s] = lo
            return carry

        lax.fori_loop(0, pg, scaled, 0, unroll=2)
        total = quadrants(jnp.dot(whl[q % 2], shl[q % 2], preferred_element_type=f32))
        sv[q] = top + jnp.log(total)
        fx[q, 0:g] = up[q] / total
        fx[q, g:] = jnp.broadcast_to(top, (8, s))


def forward(prod_child, got, w, bias, up):
    nodes = len(got)
    qd, g, s = up.shape
    pg = prod_child.shape[1]
    return pl.pallas_call(
        functools.partial(forward_kernel, nodes),
        out_shape=(
            jax.ShapeDtypeStruct((qd, g, s), f32),
            jax.ShapeDtypeStruct((qd, g + 8, s), f32),
            jax.ShapeDtypeStruct((pg, g, s), f32),
            jax.ShapeDtypeStruct((qd * pg, s), f32),
            jax.ShapeDtypeStruct((pg, s), f32),
        ),
        in_specs=[pl.BlockSpec(memory_space=SMEM)] + vmem_specs(nodes + 3),
        out_specs=tuple(vmem_specs(5)),
        scratch_shapes=[
            VMEM((got[0].shape[0] * nodes, g, s), f32),
            VMEM((2, 2 * g, pg * g), bf16),
            VMEM((2, pg * g, 2 * s), bf16),
        ],
        compiler_params=pltpu.CompilerParams(vmem_limit_bytes=20 << 20),
        cost_estimate=pl.CostEstimate(
            flops=2 * qd * 4 * g * s * pg * g, bytes_accessed=8 << 20, transcendentals=pg * g * s
        ),
        name="forward",
    )(prod_child, *got, w, bias, up)


def backward_kernel(nodes, each, prod_child, w_ref, fx, r_ref, e_ref, *refs):
    chips = nodes // CORES
    keep, give, (lf, thl, ghl) = refs[:chips], refs[chips], refs[chips + 1 :]
    qd = fx.shape[0]
    pg, g, s = e_ref.shape
    lf[...] = jnp.zeros(lf.shape, f32)

    def some(step, carry):
        for t in range(each):
            c = step * each + t
            for q in range(qd):
                at = slice(q * g, (q + 1) * g)
                hi, lo = parts(w_ref[q, c].T)
                thl[t, 0:g, at] = hi
                thl[t, g : 2 * g, at] = lo
                hi, lo = parts(fx[q, 0:g] * r_ref[pl.ds(q * pg + c, 1), :])
                ghl[t, at, 0:s] = hi
                ghl[t, at, s : 2 * s] = lo
        for t in range(each):
            c = step * each + t
            back = quadrants(jnp.dot(thl[t], ghl[t], preferred_element_type=f32))
            flow = back * e_ref[c]
            lf[prod_child[0, c]] += flow
            lf[prod_child[1, c]] += flow
        return carry

    lax.fori_loop(0, pg // each, some, 0)
    for dx in range(chips):
        k = keep[0].shape[0]
        keep[dx][...] = lf[pl.ds(node_at(dx, 0, nodes) * k, k)]
        give[dx * k : (dx + 1) * k] = lf[pl.ds(node_at(dx, 1, nodes) * k, k)]


def backward(prod_child, w, fx, r, e, nodes, ng):
    pg, g, s = e.shape
    qd = fx.shape[0]
    chips = nodes // CORES
    each = 4
    k = ng // nodes
    return pl.pallas_call(
        functools.partial(backward_kernel, nodes, each),
        out_shape=[jax.ShapeDtypeStruct((k, g, s), f32)] * chips
        + [jax.ShapeDtypeStruct((k * chips, g, s), f32)],
        in_specs=[pl.BlockSpec(memory_space=SMEM)] + vmem_specs(4),
        out_specs=vmem_specs(chips + 1),
        scratch_shapes=[
            VMEM((ng, g, s), f32),
            VMEM((each, 2 * g, qd * g), bf16),
            VMEM((each, qd * g, 2 * s), bf16),
        ],
        compiler_params=pltpu.CompilerParams(vmem_limit_bytes=20 << 20),
        cost_estimate=pl.CostEstimate(
            flops=2 * qd * 4 * g * s * pg * g, bytes_accessed=8 << 20, transcendentals=0
        ),
        name="backward",
    )(prod_child, w, fx, r, e)


def pack_kernel(*refs):
    at = 0
    for a in refs[:-1]:
        k = a.shape[0]
        refs[-1][at : at + k] = a[...]
        at += k


def pack(arrays):
    n = sum(a.shape[0] for a in arrays)
    return pl.pallas_call(
        pack_kernel,
        out_shape=jax.ShapeDtypeStruct((n,) + arrays[0].shape[1:], f32),
        in_specs=vmem_specs(len(arrays)),
        out_specs=vmem_specs(1)[0],
        compiler_params=pltpu.CompilerParams(vmem_limit_bytes=4 << 20),
        cost_estimate=pl.CostEstimate(flops=0, bytes_accessed=1 << 20, transcendentals=0),
        name="pack",
    )(*arrays)


def spread_kernel(offsets, prod_child, token, e_own, pk_own, *refs):
    pieces, (ehl, pk) = refs[: len(offsets)], refs[len(offsets) : -1]
    lv = refs[-1]
    pg, g, s = e_own.shape
    sets = lv.shape[0]
    each = pieces[0].shape[0] // sets
    nodes = lv.shape[1] // each
    for (dx, dc), piece in zip(offsets, pieces):
        src = node_at(-dx, -dc, nodes)
        for t in range(sets):
            lv[t, pl.ds(src * each, each)] = piece[t * each : (t + 1) * each]

    def product(p, carry):
        hi, lo = parts(e_own[p])
        ehl[p, 0:g, 0:s] = hi
        ehl[p, g : 2 * g, 0:s] = lo
        pk[0, pl.ds(p, 1), :] = pk_own[pl.ds(p, 1), :]
        a, b = prod_child[0, p], prod_child[1, p]
        for t in range(sets):
            x = lv[t, a] + lv[t, b]
            m = jnp.max(x, axis=0, keepdims=True)
            at = slice((t + 1) * s, (t + 2) * s)
            pk[t + 1, pl.ds(p, 1), :] = m
            hi, lo = parts(jnp.exp(x - m))
            ehl[p, 0:g, at] = hi
            ehl[p, g : 2 * g, at] = lo
        return carry

    lax.fori_loop(0, pg, product, 0, unroll=2)


def spread(prod_child, e, pk, pieces, offsets, nodes, token):
    pg, g, s = e.shape
    sets = ROWS - 1
    each = pieces[0].shape[0] // sets

    def kernel(*refs):
        spread_kernel(offsets, *refs)

    return pl.pallas_call(
        kernel,
        out_shape=(
            jax.ShapeDtypeStruct((pg, 2 * g, (sets + 1) * s), bf16),
            jax.ShapeDtypeStruct((sets + 1, pg, s), f32),
        ),
        in_specs=[pl.BlockSpec(memory_space=SMEM), pl.BlockSpec(memory_space=pl.ANY)]
        + vmem_specs(2 + len(pieces)),
        out_specs=tuple(vmem_specs(2)),
        scratch_shapes=[VMEM((sets, nodes * each, g, s), f32)],
        compiler_params=pltpu.CompilerParams(vmem_limit_bytes=20 << 20),
        cost_estimate=pl.CostEstimate(
            flops=10_000_000, bytes_accessed=10 << 20, transcendentals=pg * g * s * sets
        ),
        name="spread",
    )(prod_child, token, e, pk, *pieces)


def edges_kernel(plan, slots, count, ehl, pk, bias, *refs):
    rows = ROWS
    fxs, refs = refs[:rows], refs[rows:]
    outs, (r, lhs) = refs[1:-2], refs[-2:]
    qd, s = fxs[0].shape[0], fxs[0].shape[2]
    g = fxs[0].shape[1] - 8
    pg = pk.shape[1]
    batch = lax.axis_index("batch")
    z, y = batch // ROWS, batch % ROWS
    depth = lax.axis_size("batch") // ROWS
    for q in range(qd):
        for t in range(rows):
            top = fxs[t][q, g : g + 1]
            here = slice(q * pg, (q + 1) * pg)
            r[t, here, :] = jnp.exp((pk[t] + bias[here, :]) - top)
    for (d, k0, n, keep), out in zip(plan, outs):
        base = ((z + d + depth) % depth * ROWS + y) * keep + k0
        for k in range(n):
            b = base + k
            c, q = slots[0, b], slots[1, b]
            live = (b < count[0]).astype(f32)
            for t in range(rows):
                at = slice(t * s, (t + 1) * s)
                hi, lo = parts(fxs[t][q, 0:g] * (r[t, pl.ds(q * pg + c, 1), :] * live))
                lhs[k, 0:g, at] = hi
                lhs[k, g : 2 * g, at] = lo
        for k in range(n):
            c = slots[0, base + k]
            out[k] = quadrants(
                lax.dot_general(
                    lhs[k], ehl[c], (((1,), (1,)), ((), ())), preferred_element_type=f32
                )
            )


def edges(slots, count, ehl, pk, bias, fxs, token, plan):
    g = ehl.shape[1] // 2
    pg, width = pk.shape[1], ehl.shape[2]
    qd = fxs[0].shape[0]
    total = sum(n for _, _, n, _ in plan)

    def kernel(*refs):
        edges_kernel(plan, *refs)

    return pl.pallas_call(
        kernel,
        out_shape=[jax.ShapeDtypeStruct((n, g, g), f32) for _, _, n, _ in plan],
        in_specs=[pl.BlockSpec(memory_space=SMEM)] * 2
        + vmem_specs(3 + len(fxs))
        + [pl.BlockSpec(memory_space=pl.ANY)],
        out_specs=vmem_specs(len(plan)),
        scratch_shapes=[
            VMEM((len(fxs), qd * pg, width // len(fxs)), f32),
            VMEM((max(n for _, _, n, _ in plan), 2 * g, width), bf16),
        ],
        compiler_params=pltpu.CompilerParams(vmem_limit_bytes=20 << 20),
        cost_estimate=pl.CostEstimate(
            flops=2 * total * 4 * g * g * width, bytes_accessed=6 << 20, transcendentals=0
        ),
        name="edges",
    )(slots, count, ehl, pk, bias, *fxs, token)


def join_kernel(ap, am, bp, bm, c_ref, outp, outm):
    first = (lax.axis_index("nodes") % CORES == 0).astype(f32)
    outp[...] = (ap[...] + bp[...]) + c_ref[...] * first
    outm[...] = (am[...] + bm[...]) + c_ref[...] * (1.0 - first)


def join(ap, am, bp, bm, c):
    return pl.pallas_call(
        join_kernel,
        out_shape=[jax.ShapeDtypeStruct(ap.shape, f32)] * 2,
        in_specs=vmem_specs(5),
        out_specs=vmem_specs(2),
        compiler_params=pltpu.CompilerParams(vmem_limit_bytes=4 << 20),
        cost_estimate=pl.CostEstimate(flops=400_000, bytes_accessed=2 << 20, transcendentals=0),
        name="join",
    )(ap, am, bp, bm, c)


def near_kernel(w_hbm, a_ref, b_ref, c_ref, near, w, sem):
    keep = w.shape[0]
    own = w_hbm.at[pl.ds(lax.axis_index("batch") * keep, keep)]
    copy = pltpu.make_async_copy(own, w, sem)
    copy.start()
    copy.wait()
    near[...] = w[...] * (a_ref[...] + b_ref[...] + c_ref[...])


def weigh_near(w, a, b, c):
    return pl.pallas_call(
        near_kernel,
        out_shape=[jax.ShapeDtypeStruct(a.shape, f32)] * 2,
        in_specs=[pl.BlockSpec(memory_space=pltpu.HBM)] + vmem_specs(3),
        out_specs=vmem_specs(2),
        scratch_shapes=[pltpu.SemaphoreType.DMA],
        compiler_params=pltpu.CompilerParams(vmem_limit_bytes=50 << 20),
        cost_estimate=pl.CostEstimate(flops=200_000, bytes_accessed=1 << 20, transcendentals=0),
        name="near",
    )(w, a, b, c)


def last_kernel(near, w, a_ref, b_ref, out):
    out[...] = near[...] + w[...] * (a_ref[...] + b_ref[...])


def weigh_last(near, w, a, b):
    return pl.pallas_call(
        last_kernel,
        out_shape=jax.ShapeDtypeStruct(a.shape, f32),
        in_specs=vmem_specs(4),
        out_specs=vmem_specs(1)[0],
        compiler_params=pltpu.CompilerParams(vmem_limit_bytes=4 << 20),
        cost_estimate=pl.CostEstimate(flops=200_000, bytes_accessed=1 << 20, transcendentals=0),
        name="last",
    )(near, w, a, b)


def body(leaves, prod_child, block_weight, block_child, block_parent, block_count, upper_flow):
    prod_child = prod_child.T
    slots = jnp.concatenate([block_child, block_parent])
    nodes = lax.axis_size("nodes")
    batch = lax.axis_size("batch")
    chips, depth = nodes // CORES, batch // ROWS
    ng = leaves.shape[0] * nodes
    pg = prod_child.shape[1]
    qd = upper_flow.shape[0]
    keep = block_weight.shape[0] // batch
    far = depth // 2

    def move(a, dx=0, dc=0):
        to = lambda n: ((n // CORES + dx) % chips) * CORES + (n % CORES + dc) % CORES
        return lax.ppermute(a, "nodes", [(n, to(n)) for n in range(nodes)])

    def shift(a, dz):
        to = lambda b: ((b // ROWS + dz) % depth) * ROWS + b % ROWS
        return lax.ppermute(a, "batch", [(b, to(b)) for b in range(batch)])

    def swap(a, mask):
        return lax.ppermute(a, "batch", [(b, b ^ mask) for b in range(batch)])

    def shift_by_core(a, dz):
        pairs = []
        for n in range(nodes):
            for b in range(batch):
                z = (b // ROWS + (dz if n % CORES == 0 else -dz)) % depth
                pairs.append((n * batch + b, n * batch + z * ROWS + b % ROWS))
        return lax.ppermute(a, ("nodes", "batch"), pairs)

    def gather(a):
        out = []
        for dx in range(chips):
            got = move(a, dx) if dx else a
            out += [got, move(got, 0, 1)]
        return out

    got = gather(leaves)
    one = swap(leaves, 1)
    pair = pack([leaves, one])
    two = swap(pair, 3)
    packed = pack([one, two])
    pieces = gather(packed)

    w, bias = fold(slots, block_count, block_weight, pg, qd)
    sum_values, fx, e, r, pk = forward(prod_child, got, w, bias, upper_flow)
    fxs = [fx] + [swap(fx, t) for t in (1, 3, 2)]
    *mine, give = backward(prod_child, w, fx, r, e, nodes, ng)
    given = move(give, 0, 1)
    k = leaves.shape[0]
    flows = [a + given[dx * k : (dx + 1) * k] for dx, a in enumerate(mine)]
    ehl, pks = spread(prod_child, e, pk, pieces, hops(nodes), nodes, flows[1])

    def part(token, *ds):
        plan = [(d, 0, keep, keep) for d in ds]
        return edges(slots, block_count, ehl, pks, bias, fxs, token, plan)

    (e4,) = part(pks, far)
    r4 = shift_by_core(e4, 2)
    e3p, e3m = part(e4, 3, -3)
    r3p, r3m = shift(e3p, 1), shift(e3m, -1)
    e1p, e1m, e0 = part(e3m, 1, -1, 0)
    r1p, r1m = shift(e1p, 1), shift(e1m, -1)
    e2p, e2m = part(e1m, 2, -2)
    c2p, c2m = join(e2p, e2m, r3p, r3m, r4)
    r2p, r2m = shift(c2p, 2), shift(c2m, -2)
    leaf_flow = functools.reduce(
        jnp.add, [flows[0]] + [move(flows[dx], dx) for dx in range(1, chips)]
    )
    near, own = weigh_near(block_weight, e0, r1p, r1m)
    param_flow = weigh_last(near, own, r2p, r2m)
    return sum_values, leaf_flow, param_flow


def solution(mesh):
    placed = (
        P("nodes", None, "batch"),
        P(),
        P("nodes", None, None),
        P("nodes", None),
        P("nodes", None),
        P("nodes"),
        P("nodes", None, "batch"),
    )
    return jax.shard_map(
        body,
        mesh=mesh,
        in_specs=placed,
        out_specs=(
            P("nodes", None, "batch"),
            P("nodes", None, "batch"),
            P(("nodes", "batch"), None, None),
        ),
        check_vma=False,
    )
```

```python
import functools

import jax
import jax.numpy as jnp
from jax import lax
from jax.experimental import pallas as pl
from jax.experimental.pallas import tpu as pltpu
from jax.sharding import PartitionSpec as P


very_low = -1e30
f32, bf16 = jnp.float32, jnp.bfloat16
CORES = 2
ROWS = 4
VMEM = pltpu.VMEM
SMEM = pltpu.SMEM


def parts(x):
    hi = x.astype(bf16)
    lo = (x - hi.astype(f32)).astype(bf16)
    return hi, lo


def quadrants(x):
    g = x.shape[0] // 2
    return (x[:g, :g] + x[:g, g:]) + (x[g:, :g] + x[g:, g:])


def node_at(dx, dc, nodes):
    me = lax.axis_index("nodes")
    x, core = me // CORES, me % CORES
    chips = nodes // CORES
    return ((x + dx) % chips) * CORES + (core + dc) % CORES


def hops(nodes):
    return [(dx, dc) for dx in range(nodes // CORES) for dc in range(CORES)]


def vmem_specs(n):
    return [pl.BlockSpec(memory_space=VMEM)] * n


def fold_kernel(each, count, slots_any, w_hbm, acc, bias, w, slots, sems, sem):
    pg = acc.shape[1]
    steps = w.shape[0] // each
    index = pltpu.make_async_copy(slots_any, slots, sem)
    index.start()
    copies = []
    for j in range(steps):
        at = pl.ds(j * each, each)
        copies.append(pltpu.make_async_copy(w_hbm.at[at], w.at[at], sems.at[j]))
        copies[j].start()

    bias[...] = jnp.full(bias.shape, very_low, f32)

    def clear(c, carry):
        for q in range(acc.shape[0]):
            acc[q, c] = jnp.zeros(acc.shape[2:], f32)
        return carry

    lax.fori_loop(0, pg, clear, 0)
    index.wait()
    for j in range(steps):
        copies[j].wait()

        def add(t, carry, j=j):
            b = j * each + t
            c, q = slots[0, b], slots[1, b]
            live = b < count[0]
            acc[q, c] += w[b] * live.astype(f32)
            row = pl.ds(q * pg + c, 1)
            bias[row, :] = jnp.where(live, 0.0, bias[row, :])
            return carry

        lax.fori_loop(0, each, add, 0, unroll=4)


def fold(slots, block_count, block_weight, pg, qd):
    blocks, g, _ = block_weight.shape
    each = 16
    return pl.pallas_call(
        functools.partial(fold_kernel, each),
        out_shape=(
            jax.ShapeDtypeStruct((qd, pg, g, g), f32),
            jax.ShapeDtypeStruct((qd * pg, g), f32),
        ),
        in_specs=[
            pl.BlockSpec(memory_space=SMEM),
            pl.BlockSpec(memory_space=pl.ANY),
            pl.BlockSpec(memory_space=pltpu.HBM),
        ],
        out_specs=tuple(vmem_specs(2)),
        scratch_shapes=[
            VMEM((blocks, g, g), f32),
            SMEM(slots.shape, jnp.int32),
            pltpu.SemaphoreType.DMA((blocks // each,)),
            pltpu.SemaphoreType.DMA,
        ],
        compiler_params=pltpu.CompilerParams(vmem_limit_bytes=46 << 20),
        cost_estimate=pl.CostEstimate(flops=20_000_000, bytes_accessed=16 << 20, transcendentals=0),
        name="fold",
    )(block_count, slots, block_weight)


def forward_kernel(nodes, prod_child, *refs):
    n = nodes
    got = refs[:n]
    w_ref, bias, up, sv_hbm, fx, e_ref, r_ref, pk, lv, whl, shl, sv, sems = refs[n:]
    pg, g, s = e_ref.shape
    qd = up.shape[0]
    each = lv.shape[0] // n
    for k, (dx, dc) in enumerate(hops(n)):
        src = node_at(-dx, -dc, n)
        lv[pl.ds(src * each, each)] = got[k][0:each]

    def product(p, carry):
        x = lv[prod_child[0, p]] + lv[prod_child[1, p]]
        m = jnp.max(x, axis=0, keepdims=True)
        pk[pl.ds(p, 1), :] = m
        e_ref[p] = jnp.exp(x - m)
        return carry

    lax.fori_loop(0, pg, product, 0, unroll=2)
    tops = []
    for q in range(qd):
        here = slice(q * pg, (q + 1) * pg)
        biased = pk[...] + bias[here]
        top = jnp.max(biased, axis=0, keepdims=True)
        r_ref[here] = jnp.exp(biased - top)
        tops.append(top)

    def scaled(q):
        for c in range(pg):
            at = slice(c * g, (c + 1) * g)
            hi, lo = parts(w_ref[q, c])
            whl[q % 2, 0:g, at] = hi
            whl[q % 2, g : 2 * g, at] = lo
            k = q * pg + c
            hi, lo = parts(e_ref[c] * r_ref[k : k + 1, :])
            shl[q % 2, at, 0:s] = hi
            shl[q % 2, at, s : 2 * s] = lo

    scaled(0)
    copies = []
    for q in range(qd):
        total = quadrants(jnp.dot(whl[q % 2], shl[q % 2], preferred_element_type=f32))
        if q + 1 < qd:
            scaled(q + 1)
        sv[q] = tops[q] + jnp.log(total)
        fx[q, 0:g] = up[q] / total
        fx[q, g:] = jnp.broadcast_to(tops[q], (8, s))
        copies.append(pltpu.make_async_copy(sv.at[q], sv_hbm.at[q], sems.at[q]))
        if q > 0:
            copies[q - 1].start()
    copies[-1].start()
    for copy in copies:
        copy.wait()


def forward(prod_child, got, w, bias, up, ng):
    nodes = len(got)
    qd, g, s = up.shape
    pg = prod_child.shape[1]
    return pl.pallas_call(
        functools.partial(forward_kernel, nodes),
        out_shape=(
            jax.ShapeDtypeStruct((qd, g, s), f32),
            jax.ShapeDtypeStruct((qd, g + 8, s), f32),
            jax.ShapeDtypeStruct((pg, g, s), f32),
            jax.ShapeDtypeStruct((qd * pg, s), f32),
            jax.ShapeDtypeStruct((pg, s), f32),
        ),
        in_specs=[pl.BlockSpec(memory_space=SMEM)] + vmem_specs(nodes + 3),
        out_specs=(pl.BlockSpec(memory_space=pltpu.HBM), *vmem_specs(4)),
        scratch_shapes=[
            VMEM((ng, g, s), f32),
            VMEM((2, 2 * g, pg * g), bf16),
            VMEM((2, pg * g, 2 * s), bf16),
            VMEM((qd, g, s), f32),
            pltpu.SemaphoreType.DMA((qd,)),
        ],
        compiler_params=pltpu.CompilerParams(vmem_limit_bytes=20 << 20),
        cost_estimate=pl.CostEstimate(
            flops=2 * qd * 4 * g * s * pg * g, bytes_accessed=8 << 20, transcendentals=pg * g * s
        ),
        name="forward",
    )(prod_child, *got, w, bias, up)


def backward_kernel(nodes, each, prod_child, w_ref, fx, r_ref, e_ref, *refs):
    chips = nodes // CORES
    keep, give, (lf, thl, ghl) = refs[:chips], refs[chips], refs[chips + 1 :]
    qd = fx.shape[0]
    pg, g, s = e_ref.shape
    lf[...] = jnp.zeros(lf.shape, f32)

    def some(step, carry):
        for t in range(each):
            c = step * each + t
            for q in range(qd):
                at = slice(q * g, (q + 1) * g)
                hi, lo = parts(w_ref[q, c].T)
                thl[t, 0:g, at] = hi
                thl[t, g : 2 * g, at] = lo
                hi, lo = parts(fx[q, 0:g] * r_ref[pl.ds(q * pg + c, 1), :])
                ghl[t, at, 0:s] = hi
                ghl[t, at, s : 2 * s] = lo
        for t in range(each):
            c = step * each + t
            back = quadrants(jnp.dot(thl[t], ghl[t], preferred_element_type=f32))
            flow = back * e_ref[c]
            lf[prod_child[0, c]] += flow
            lf[prod_child[1, c]] += flow
        return carry

    lax.fori_loop(0, pg // each, some, 0)
    for dx in range(chips):
        k = keep[0].shape[0]
        keep[dx][...] = lf[pl.ds(node_at(dx, 0, nodes) * k, k)]
        give[dx * k : (dx + 1) * k] = lf[pl.ds(node_at(dx, 1, nodes) * k, k)]


def backward(prod_child, w, fx, r, e, nodes, ng):
    pg, g, s = e.shape
    qd = fx.shape[0]
    chips = nodes // CORES
    each = 4
    k = ng // nodes
    return pl.pallas_call(
        functools.partial(backward_kernel, nodes, each),
        out_shape=[jax.ShapeDtypeStruct((k, g, s), f32)] * chips
        + [jax.ShapeDtypeStruct((k * chips, g, s), f32)],
        in_specs=[pl.BlockSpec(memory_space=SMEM)] + vmem_specs(4),
        out_specs=vmem_specs(chips + 1),
        scratch_shapes=[
            VMEM((ng, g, s), f32),
            VMEM((each, 2 * g, qd * g), bf16),
            VMEM((each, qd * g, 2 * s), bf16),
        ],
        compiler_params=pltpu.CompilerParams(vmem_limit_bytes=20 << 20),
        cost_estimate=pl.CostEstimate(
            flops=2 * qd * 4 * g * s * pg * g, bytes_accessed=8 << 20, transcendentals=0
        ),
        name="backward",
    )(prod_child, w, fx, r, e)


def pack_kernel(*refs):
    at = 0
    for a in refs[:-1]:
        k = a.shape[0]
        refs[-1][at : at + k] = a[...]
        at += k


def pack(arrays):
    n = sum(a.shape[0] for a in arrays)
    return pl.pallas_call(
        pack_kernel,
        out_shape=jax.ShapeDtypeStruct((n,) + arrays[0].shape[1:], f32),
        in_specs=vmem_specs(len(arrays)),
        out_specs=vmem_specs(1)[0],
        compiler_params=pltpu.CompilerParams(vmem_limit_bytes=4 << 20),
        cost_estimate=pl.CostEstimate(flops=0, bytes_accessed=1 << 20, transcendentals=0),
        name="pack",
    )(*arrays)


def spread_kernel(offsets, prod_child, token, e_own, pk_own, *refs):
    pieces, (ehl, pk) = refs[: len(offsets)], refs[len(offsets) : -1]
    lv = refs[-1]
    pg, g, s = e_own.shape
    sets = lv.shape[0]
    each = pieces[0].shape[0] // sets
    nodes = lv.shape[1] // each
    for (dx, dc), piece in zip(offsets, pieces):
        src = node_at(-dx, -dc, nodes)
        for t in range(sets):
            lv[t, pl.ds(src * each, each)] = piece[t * each : (t + 1) * each]

    def product(p, carry):
        hi, lo = parts(e_own[p])
        ehl[p, 0:g, 0:s] = hi
        ehl[p, g : 2 * g, 0:s] = lo
        pk[0, pl.ds(p, 1), :] = pk_own[pl.ds(p, 1), :]
        a, b = prod_child[0, p], prod_child[1, p]
        for t in range(sets):
            x = lv[t, a] + lv[t, b]
            m = jnp.max(x, axis=0, keepdims=True)
            at = slice((t + 1) * s, (t + 2) * s)
            pk[t + 1, pl.ds(p, 1), :] = m
            hi, lo = parts(jnp.exp(x - m))
            ehl[p, 0:g, at] = hi
            ehl[p, g : 2 * g, at] = lo
        return carry

    lax.fori_loop(0, pg, product, 0, unroll=2)


def spread(prod_child, e, pk, pieces, offsets, nodes, token):
    pg, g, s = e.shape
    sets = ROWS - 1
    each = pieces[0].shape[0] // sets

    def kernel(*refs):
        spread_kernel(offsets, *refs)

    return pl.pallas_call(
        kernel,
        out_shape=(
            jax.ShapeDtypeStruct((pg, 2 * g, (sets + 1) * s), bf16),
            jax.ShapeDtypeStruct((sets + 1, pg, s), f32),
        ),
        in_specs=[pl.BlockSpec(memory_space=SMEM), pl.BlockSpec(memory_space=pl.ANY)]
        + vmem_specs(2 + len(pieces)),
        out_specs=tuple(vmem_specs(2)),
        scratch_shapes=[VMEM((sets, nodes * each, g, s), f32)],
        compiler_params=pltpu.CompilerParams(vmem_limit_bytes=20 << 20),
        cost_estimate=pl.CostEstimate(
            flops=10_000_000, bytes_accessed=10 << 20, transcendentals=pg * g * s * sets
        ),
        name="spread",
    )(prod_child, token, e, pk, *pieces)


def edges_kernel(plan, slots, count, ehl, pk, bias, *refs):
    rows = ROWS
    fxs, refs = refs[:rows], refs[rows:]
    outs, (r, lhs) = refs[1:-2], refs[-2:]
    qd, s = fxs[0].shape[0], fxs[0].shape[2]
    g = fxs[0].shape[1] - 8
    pg = pk.shape[1]
    batch = lax.axis_index("batch")
    z, y = batch // ROWS, batch % ROWS
    depth = lax.axis_size("batch") // ROWS
    for q in range(qd):
        for t in range(rows):
            top = fxs[t][q, g : g + 1]
            here = slice(q * pg, (q + 1) * pg)
            r[t, here, :] = jnp.exp((pk[t] + bias[here, :]) - top)
    for ds, out in zip(plan, outs):
        keep = out.shape[0] // len(ds)
        places = []
        for d in ds:
            first = ((z + d + depth) % depth * ROWS + y) * keep
            places += [first + k for k in range(keep)]
        for k, b in enumerate(places):
            c, q = slots[0, b], slots[1, b]
            live = (b < count[0]).astype(f32)
            for t in range(rows):
                at = slice(t * s, (t + 1) * s)
                hi, lo = parts(fxs[t][q, 0:g] * (r[t, pl.ds(q * pg + c, 1), :] * live))
                lhs[k, 0:g, at] = hi
                lhs[k, g : 2 * g, at] = lo
        for k, b in enumerate(places):
            c = slots[0, b]
            out[k] = quadrants(
                lax.dot_general(
                    lhs[k], ehl[c], (((1,), (1,)), ((), ())), preferred_element_type=f32
                )
            )


def edges(slots, count, ehl, pk, bias, fxs, token, plan, keep):
    g = ehl.shape[1] // 2
    pg, width = pk.shape[1], ehl.shape[2]
    qd = fxs[0].shape[0]
    counts = [keep * len(ds) for ds in plan]

    def kernel(*refs):
        edges_kernel(plan, *refs)

    return pl.pallas_call(
        kernel,
        out_shape=[jax.ShapeDtypeStruct((n, g, g), f32) for n in counts],
        in_specs=[pl.BlockSpec(memory_space=SMEM)] * 2
        + vmem_specs(3 + len(fxs))
        + [pl.BlockSpec(memory_space=pl.ANY)],
        out_specs=vmem_specs(len(plan)),
        scratch_shapes=[
            VMEM((len(fxs), qd * pg, width // len(fxs)), f32),
            VMEM((max(counts), 2 * g, width), bf16),
        ],
        compiler_params=pltpu.CompilerParams(vmem_limit_bytes=20 << 20),
        cost_estimate=pl.CostEstimate(
            flops=2 * sum(counts) * 4 * g * g * width, bytes_accessed=6 << 20, transcendentals=0
        ),
        name="edges",
    )(slots, count, ehl, pk, bias, *fxs, token)


def join_kernel(ap, am, bp, bm, c_ref, outp, outm):
    first = (lax.axis_index("nodes") % CORES == 0).astype(f32)
    n = ap.shape[0]
    outp[...] = (ap[...] + bp[0:n]) + c_ref[...] * first
    outm[...] = (am[...] + bm[0:n]) + c_ref[...] * (1.0 - first)


def join(ap, am, bp, bm, c):
    return pl.pallas_call(
        join_kernel,
        out_shape=[jax.ShapeDtypeStruct(ap.shape, f32)] * 2,
        in_specs=vmem_specs(5),
        out_specs=vmem_specs(2),
        compiler_params=pltpu.CompilerParams(vmem_limit_bytes=4 << 20),
        cost_estimate=pl.CostEstimate(flops=400_000, bytes_accessed=2 << 20, transcendentals=0),
        name="join",
    )(ap, am, bp, bm, c)


def near_kernel(w_hbm, a_ref, b_ref, c_ref, near, w, sem):
    keep = w.shape[0]
    own = w_hbm.at[pl.ds(lax.axis_index("batch") * keep, keep)]
    copy = pltpu.make_async_copy(own, w, sem)
    copy.start()
    copy.wait()
    near[...] = w[...] * (a_ref[...] + b_ref[keep:] + c_ref[keep:])


def weigh_near(w, a, b, c):
    return pl.pallas_call(
        near_kernel,
        out_shape=[jax.ShapeDtypeStruct(a.shape, f32)] * 2,
        in_specs=[pl.BlockSpec(memory_space=pltpu.HBM)] + vmem_specs(3),
        out_specs=vmem_specs(2),
        scratch_shapes=[pltpu.SemaphoreType.DMA],
        compiler_params=pltpu.CompilerParams(vmem_limit_bytes=50 << 20),
        cost_estimate=pl.CostEstimate(flops=200_000, bytes_accessed=1 << 20, transcendentals=0),
        name="near",
    )(w, a, b, c)


def last_kernel(near, w, a_ref, b_ref, out):
    out[...] = near[...] + w[...] * (a_ref[...] + b_ref[...])


def weigh_last(near, w, a, b):
    return pl.pallas_call(
        last_kernel,
        out_shape=jax.ShapeDtypeStruct(a.shape, f32),
        in_specs=vmem_specs(4),
        out_specs=vmem_specs(1)[0],
        compiler_params=pltpu.CompilerParams(vmem_limit_bytes=4 << 20),
        cost_estimate=pl.CostEstimate(flops=200_000, bytes_accessed=1 << 20, transcendentals=0),
        name="last",
    )(near, w, a, b)


def body(leaves, prod_child, block_weight, block_child, block_parent, block_count, upper_flow):
    prod_child = prod_child.T
    slots = jnp.concatenate([block_child, block_parent])
    nodes = lax.axis_size("nodes")
    batch = lax.axis_size("batch")
    chips, depth = nodes // CORES, batch // ROWS
    ng = leaves.shape[0] * nodes
    pg = prod_child.shape[1]
    qd = upper_flow.shape[0]
    keep = block_weight.shape[0] // batch
    far = depth // 2

    def move(a, dx=0, dc=0):
        to = lambda n: ((n // CORES + dx) % chips) * CORES + (n % CORES + dc) % CORES
        return lax.ppermute(a, "nodes", [(n, to(n)) for n in range(nodes)])

    def shift(a, dz):
        to = lambda b: ((b // ROWS + dz) % depth) * ROWS + b % ROWS
        return lax.ppermute(a, "batch", [(b, to(b)) for b in range(batch)])

    def swap(a, mask):
        return lax.ppermute(a, "batch", [(b, b ^ mask) for b in range(batch)])

    def shift_by_core(a, dz):
        pairs = []
        for n in range(nodes):
            for b in range(batch):
                z = (b // ROWS + (dz if n % CORES == 0 else -dz)) % depth
                pairs.append((n * batch + b, n * batch + z * ROWS + b % ROWS))
        return lax.ppermute(a, ("nodes", "batch"), pairs)

    def gather(a):
        out = []
        for dx in range(chips):
            got = move(a, dx) if dx else a
            out += [got, move(got, 0, 1)]
        return out

    got = gather(leaves)
    one = swap(leaves, 1)
    pair = pack([leaves, one])
    two = swap(pair, 3)
    packed = pack([one, two])
    pieces = gather(packed)

    w, bias = fold(slots, block_count, block_weight, pg, qd)
    sum_values, fx, e, r, pk = forward(prod_child, [pair] + got[1:], w, bias, upper_flow, ng)
    fxs = [fx] + [swap(fx, t) for t in (1, 3, 2)]
    *mine, give = backward(prod_child, w, fx, r, e, nodes, ng)
    given = move(give, 0, 1)
    k = leaves.shape[0]
    flows = [a + given[dx * k : (dx + 1) * k] for dx, a in enumerate(mine)]
    ehl, pks = spread(prod_child, e, pk, pieces, hops(nodes), nodes, flows[1])

    def part(token, *plan):
        return edges(slots, block_count, ehl, pks, bias, fxs, token, plan, keep)

    (e4,) = part(pks, (far,))
    r4 = shift_by_core(e4, 2)
    (ep,) = part(e4, (3, 1))
    rp = shift(ep, 1)
    (em,) = part(ep, (-3, -1))
    rm = shift(em, -1)
    e2p, e2m, e0 = part(em, (2,), (-2,), (0,))
    c2p, c2m = join(e2p, e2m, rp, rm, r4)
    r2p, r2m = shift(c2p, 2), shift(c2m, -2)
    leaf_flow = functools.reduce(
        jnp.add, [flows[0]] + [move(flows[dx], dx) for dx in range(1, chips)]
    )
    near, own = weigh_near(block_weight, e0, rp, rm)
    param_flow = weigh_last(near, own, r2p, r2m)
    return sum_values, leaf_flow, param_flow


def solution(mesh):
    placed = (
        P("nodes", None, "batch"),
        P(),
        P("nodes", None, None),
        P("nodes", None),
        P("nodes", None),
        P("nodes"),
        P("nodes", None, "batch"),
    )
    return jax.shard_map(
        body,
        mesh=mesh,
        in_specs=placed,
        out_specs=(
            P("nodes", None, "batch"),
            P("nodes", None, "batch"),
            P(("nodes", "batch"), None, None),
        ),
        check_vma=False,
    )
```

```python
import functools

import jax
import jax.numpy as jnp
from jax import lax
from jax.experimental import pallas as pl
from jax.experimental.pallas import tpu as pltpu
from jax.sharding import PartitionSpec as P


very_low = -1e30
f32, bf16 = jnp.float32, jnp.bfloat16
CORES = 2
ROWS = 4
VMEM = pltpu.VMEM
SMEM = pltpu.SMEM


def parts(x):
    hi = x.astype(bf16)
    lo = (x - hi.astype(f32)).astype(bf16)
    return hi, lo


def quadrants(x):
    g = x.shape[0] // 2
    return (x[:g, :g] + x[:g, g:]) + (x[g:, :g] + x[g:, g:])


def node_at(dx, dc, nodes):
    me = lax.axis_index("nodes")
    x, core = me // CORES, me % CORES
    chips = nodes // CORES
    return ((x + dx) % chips) * CORES + (core + dc) % CORES


def hops(nodes):
    return [(dx, dc) for dx in range(nodes // CORES) for dc in range(CORES)]


def vmem_specs(n):
    return [pl.BlockSpec(memory_space=VMEM)] * n


def fold_kernel(each, count, slots_any, w_hbm, acc, bias, w, slots, sems, sem):
    pg = acc.shape[1]
    steps = w.shape[0] // each
    index = pltpu.make_async_copy(slots_any, slots, sem)
    index.start()
    copies = []
    for j in range(steps):
        at = pl.ds(j * each, each)
        copies.append(pltpu.make_async_copy(w_hbm.at[at], w.at[at], sems.at[j]))
        copies[j].start()

    bias[...] = jnp.full(bias.shape, very_low, f32)

    def clear(c, carry):
        for q in range(acc.shape[0]):
            acc[q, c] = jnp.zeros(acc.shape[2:], f32)
        return carry

    lax.fori_loop(0, pg, clear, 0)
    index.wait()
    for j in range(steps):
        copies[j].wait()

        def add(t, carry, j=j):
            b = j * each + t
            c, q = slots[0, b], slots[1, b]
            live = b < count[0]
            acc[q, c] += w[b] * live.astype(f32)
            row = pl.ds(q * pg + c, 1)
            bias[row, :] = jnp.where(live, 0.0, bias[row, :])
            return carry

        lax.fori_loop(0, each, add, 0, unroll=4)


def fold(slots, block_count, block_weight, pg, qd):
    blocks, g, _ = block_weight.shape
    each = 16
    return pl.pallas_call(
        functools.partial(fold_kernel, each),
        out_shape=(
            jax.ShapeDtypeStruct((qd, pg, g, g), f32),
            jax.ShapeDtypeStruct((qd * pg, g), f32),
        ),
        in_specs=[
            pl.BlockSpec(memory_space=SMEM),
            pl.BlockSpec(memory_space=pl.ANY),
            pl.BlockSpec(memory_space=pltpu.HBM),
        ],
        out_specs=tuple(vmem_specs(2)),
        scratch_shapes=[
            VMEM((blocks, g, g), f32),
            SMEM(slots.shape, jnp.int32),
            pltpu.SemaphoreType.DMA((blocks // each,)),
            pltpu.SemaphoreType.DMA,
        ],
        compiler_params=pltpu.CompilerParams(vmem_limit_bytes=46 << 20),
        cost_estimate=pl.CostEstimate(flops=20_000_000, bytes_accessed=16 << 20, transcendentals=0),
        name="fold",
    )(block_count, slots, block_weight)


def forward_kernel(nodes, prod_child, *refs):
    n = nodes
    got = refs[:n]
    w_ref, bias, up, sv_hbm, fx, e_ref, r_ref, pk, lv, whl, shl, sv, sems = refs[n:]
    pg, g, s = e_ref.shape
    qd = up.shape[0]
    each = lv.shape[0] // n
    for k, (dx, dc) in enumerate(hops(n)):
        src = node_at(-dx, -dc, n)
        lv[pl.ds(src * each, each)] = got[k][0:each]

    def product(p, carry):
        x = lv[prod_child[0, p]] + lv[prod_child[1, p]]
        m = jnp.max(x, axis=0, keepdims=True)
        pk[pl.ds(p, 1), :] = m
        e_ref[p] = jnp.exp(x - m)
        return carry

    lax.fori_loop(0, pg, product, 0, unroll=2)
    tops = []
    for q in range(qd):
        here = slice(q * pg, (q + 1) * pg)
        biased = pk[...] + bias[here]
        top = jnp.max(biased, axis=0, keepdims=True)
        r_ref[here] = jnp.exp(biased - top)
        tops.append(top)

    def scaled(q):
        for c in range(pg):
            at = slice(c * g, (c + 1) * g)
            hi, lo = parts(w_ref[q, c])
            whl[q % 2, 0:g, at] = hi
            whl[q % 2, g : 2 * g, at] = lo
            k = q * pg + c
            hi, lo = parts(e_ref[c] * r_ref[k : k + 1, :])
            shl[q % 2, at, 0:s] = hi
            shl[q % 2, at, s : 2 * s] = lo

    scaled(0)
    copies = []
    for q in range(qd):
        total = quadrants(jnp.dot(whl[q % 2], shl[q % 2], preferred_element_type=f32))
        if q + 1 < qd:
            scaled(q + 1)
        sv[q] = tops[q] + jnp.log(total)
        fx[q] = up[q] / total
        copies.append(pltpu.make_async_copy(sv.at[q], sv_hbm.at[q], sems.at[q]))
        if q > 0:
            copies[q - 1].start()
    copies[-1].start()
    for copy in copies:
        copy.wait()


def forward(prod_child, got, w, bias, up, ng):
    nodes = len(got)
    qd, g, s = up.shape
    pg = prod_child.shape[1]
    return pl.pallas_call(
        functools.partial(forward_kernel, nodes),
        out_shape=(
            jax.ShapeDtypeStruct((qd, g, s), f32),
            jax.ShapeDtypeStruct((qd, g, s), f32),
            jax.ShapeDtypeStruct((pg, g, s), f32),
            jax.ShapeDtypeStruct((qd * pg, s), f32),
            jax.ShapeDtypeStruct((pg, s), f32),
        ),
        in_specs=[pl.BlockSpec(memory_space=SMEM)] + vmem_specs(nodes + 3),
        out_specs=(pl.BlockSpec(memory_space=pltpu.HBM), *vmem_specs(4)),
        scratch_shapes=[
            VMEM((ng, g, s), f32),
            VMEM((2, 2 * g, pg * g), bf16),
            VMEM((2, pg * g, 2 * s), bf16),
            VMEM((qd, g, s), f32),
            pltpu.SemaphoreType.DMA((qd,)),
        ],
        compiler_params=pltpu.CompilerParams(vmem_limit_bytes=20 << 20),
        cost_estimate=pl.CostEstimate(
            flops=2 * qd * 4 * g * s * pg * g, bytes_accessed=8 << 20, transcendentals=pg * g * s
        ),
        name="forward",
    )(prod_child, *got, w, bias, up)


def backward_kernel(nodes, each, prod_child, w_ref, fx, r_ref, e_ref, *refs):
    chips = nodes // CORES
    keep, give, (lf, thl, ghl) = refs[:chips], refs[chips], refs[chips + 1 :]
    qd = fx.shape[0]
    pg, g, s = e_ref.shape
    lf[...] = jnp.zeros(lf.shape, f32)

    def some(step, carry):
        for t in range(each):
            c = step * each + t
            for q in range(qd):
                at = slice(q * g, (q + 1) * g)
                hi, lo = parts(w_ref[q, c].T)
                thl[t, 0:g, at] = hi
                thl[t, g : 2 * g, at] = lo
                hi, lo = parts(fx[q] * r_ref[pl.ds(q * pg + c, 1), :])
                ghl[t, at, 0:s] = hi
                ghl[t, at, s : 2 * s] = lo
        for t in range(each):
            c = step * each + t
            back = quadrants(jnp.dot(thl[t], ghl[t], preferred_element_type=f32))
            flow = back * e_ref[c]
            lf[prod_child[0, c]] += flow
            lf[prod_child[1, c]] += flow
        return carry

    lax.fori_loop(0, pg // each, some, 0)
    for dx in range(chips):
        k = keep[0].shape[0]
        keep[dx][...] = lf[pl.ds(node_at(dx, 0, nodes) * k, k)]
        give[dx * k : (dx + 1) * k] = lf[pl.ds(node_at(dx, 1, nodes) * k, k)]


def backward(prod_child, w, fx, r, e, nodes, ng):
    pg, g, s = e.shape
    qd = fx.shape[0]
    chips = nodes // CORES
    each = 4
    k = ng // nodes
    return pl.pallas_call(
        functools.partial(backward_kernel, nodes, each),
        out_shape=[jax.ShapeDtypeStruct((k, g, s), f32)] * chips
        + [jax.ShapeDtypeStruct((k * chips, g, s), f32)],
        in_specs=[pl.BlockSpec(memory_space=SMEM)] + vmem_specs(4),
        out_specs=vmem_specs(chips + 1),
        scratch_shapes=[
            VMEM((ng, g, s), f32),
            VMEM((each, 2 * g, qd * g), bf16),
            VMEM((each, qd * g, 2 * s), bf16),
        ],
        compiler_params=pltpu.CompilerParams(vmem_limit_bytes=20 << 20),
        cost_estimate=pl.CostEstimate(
            flops=2 * qd * 4 * g * s * pg * g, bytes_accessed=8 << 20, transcendentals=0
        ),
        name="backward",
    )(prod_child, w, fx, r, e)


def pack_kernel(*refs):
    at = 0
    for a in refs[:-1]:
        k = a.shape[0]
        refs[-1][at : at + k] = a[...]
        at += k


def pack(arrays):
    n = sum(a.shape[0] for a in arrays)
    return pl.pallas_call(
        pack_kernel,
        out_shape=jax.ShapeDtypeStruct((n,) + arrays[0].shape[1:], f32),
        in_specs=vmem_specs(len(arrays)),
        out_specs=vmem_specs(1)[0],
        compiler_params=pltpu.CompilerParams(vmem_limit_bytes=4 << 20),
        cost_estimate=pl.CostEstimate(flops=0, bytes_accessed=1 << 20, transcendentals=0),
        name="pack",
    )(*arrays)


def spread_kernel(offsets, prod_child, token, e_own, pk_own, *refs):
    pieces, (ehl, pk) = refs[: len(offsets)], refs[len(offsets) : -1]
    lv = refs[-1]
    pg, g, s = e_own.shape
    sets = lv.shape[0]
    each = pieces[0].shape[0] // sets
    nodes = lv.shape[1] // each
    for (dx, dc), piece in zip(offsets, pieces):
        src = node_at(-dx, -dc, nodes)
        for t in range(sets):
            lv[t, pl.ds(src * each, each)] = piece[t * each : (t + 1) * each]

    def product(p, carry):
        hi, lo = parts(e_own[p])
        ehl[p, 0:g, 0:s] = hi
        ehl[p, g : 2 * g, 0:s] = lo
        pk[0, pl.ds(p, 1), :] = pk_own[pl.ds(p, 1), :]
        a, b = prod_child[0, p], prod_child[1, p]
        for t in range(sets):
            x = lv[t, a] + lv[t, b]
            m = jnp.max(x, axis=0, keepdims=True)
            at = slice((t + 1) * s, (t + 2) * s)
            pk[t + 1, pl.ds(p, 1), :] = m
            hi, lo = parts(jnp.exp(x - m))
            ehl[p, 0:g, at] = hi
            ehl[p, g : 2 * g, at] = lo
        return carry

    lax.fori_loop(0, pg, product, 0, unroll=2)


def spread(prod_child, e, pk, pieces, offsets, nodes, token):
    pg, g, s = e.shape
    sets = ROWS - 1
    each = pieces[0].shape[0] // sets

    def kernel(*refs):
        spread_kernel(offsets, *refs)

    return pl.pallas_call(
        kernel,
        out_shape=(
            jax.ShapeDtypeStruct((pg, 2 * g, (sets + 1) * s), bf16),
            jax.ShapeDtypeStruct((sets + 1, pg, s), f32),
        ),
        in_specs=[pl.BlockSpec(memory_space=SMEM), pl.BlockSpec(memory_space=pl.ANY)]
        + vmem_specs(2 + len(pieces)),
        out_specs=tuple(vmem_specs(2)),
        scratch_shapes=[VMEM((sets, nodes * each, g, s), f32)],
        compiler_params=pltpu.CompilerParams(vmem_limit_bytes=20 << 20),
        cost_estimate=pl.CostEstimate(
            flops=10_000_000, bytes_accessed=10 << 20, transcendentals=pg * g * s * sets
        ),
        name="spread",
    )(prod_child, token, e, pk, *pieces)


def edges_kernel(plan, slots, count, ehl, pk, bias, *refs):
    rows = ROWS
    fxs, refs = refs[:rows], refs[rows:]
    outs, (r, lhs) = refs[1:-2], refs[-2:]
    qd, s = fxs[0].shape[0], fxs[0].shape[2]
    g = fxs[0].shape[1]
    pg = pk.shape[1]
    batch = lax.axis_index("batch")
    z, y = batch // ROWS, batch % ROWS
    depth = lax.axis_size("batch") // ROWS
    for q in range(qd):
        for t in range(rows):
            here = slice(q * pg, (q + 1) * pg)
            biased = pk[t] + bias[here, :]
            r[t, here, :] = jnp.exp(biased - jnp.max(biased, axis=0, keepdims=True))
    for ds, out in zip(plan, outs):
        keep = out.shape[0] // len(ds)
        places = []
        for d in ds:
            first = ((z + d + depth) % depth * ROWS + y) * keep
            places += [first + k for k in range(keep)]
        for k, b in enumerate(places):
            c, q = slots[0, b], slots[1, b]
            live = (b < count[0]).astype(f32)
            for t in range(rows):
                at = slice(t * s, (t + 1) * s)
                hi, lo = parts(fxs[t][q] * (r[t, pl.ds(q * pg + c, 1), :] * live))
                lhs[k, 0:g, at] = hi
                lhs[k, g : 2 * g, at] = lo
        for k, b in enumerate(places):
            c = slots[0, b]
            out[k] = quadrants(
                lax.dot_general(
                    lhs[k], ehl[c], (((1,), (1,)), ((), ())), preferred_element_type=f32
                )
            )


def edges(slots, count, ehl, pk, bias, fxs, token, plan, keep):
    g = ehl.shape[1] // 2
    pg, width = pk.shape[1], ehl.shape[2]
    qd = fxs[0].shape[0]
    counts = [keep * len(ds) for ds in plan]

    def kernel(*refs):
        edges_kernel(plan, *refs)

    return pl.pallas_call(
        kernel,
        out_shape=[jax.ShapeDtypeStruct((n, g, g), f32) for n in counts],
        in_specs=[pl.BlockSpec(memory_space=SMEM)] * 2
        + vmem_specs(3 + len(fxs))
        + [pl.BlockSpec(memory_space=pl.ANY)],
        out_specs=vmem_specs(len(plan)),
        scratch_shapes=[
            VMEM((len(fxs), qd * pg, width // len(fxs)), f32),
            VMEM((max(counts), 2 * g, width), bf16),
        ],
        compiler_params=pltpu.CompilerParams(vmem_limit_bytes=20 << 20),
        cost_estimate=pl.CostEstimate(
            flops=2 * sum(counts) * 4 * g * g * width, bytes_accessed=6 << 20, transcendentals=0
        ),
        name="edges",
    )(slots, count, ehl, pk, bias, *fxs, token)


def join_kernel(ap, am, bp, bm, c_ref, outp, outm):
    first = (lax.axis_index("nodes") % CORES == 0).astype(f32)
    outp[...] = (ap[...] + bp[...]) + c_ref[...] * first
    outm[...] = (am[...] + bm[...]) + c_ref[...] * (1.0 - first)


def join(ap, am, bp, bm, c):
    return pl.pallas_call(
        join_kernel,
        out_shape=[jax.ShapeDtypeStruct(ap.shape, f32)] * 2,
        in_specs=vmem_specs(5),
        out_specs=vmem_specs(2),
        compiler_params=pltpu.CompilerParams(vmem_limit_bytes=4 << 20),
        cost_estimate=pl.CostEstimate(flops=400_000, bytes_accessed=2 << 20, transcendentals=0),
        name="join",
    )(ap, am, bp, bm, c)


def near_kernel(w_hbm, a_ref, near, w, sem):
    keep = w.shape[0]
    own = w_hbm.at[pl.ds(lax.axis_index("batch") * keep, keep)]
    copy = pltpu.make_async_copy(own, w, sem)
    copy.start()
    copy.wait()
    near[...] = w[...] * a_ref[...]


def weigh_near(w, a):
    return pl.pallas_call(
        near_kernel,
        out_shape=[jax.ShapeDtypeStruct(a.shape, f32)] * 2,
        in_specs=[pl.BlockSpec(memory_space=pltpu.HBM)] + vmem_specs(1),
        out_specs=vmem_specs(2),
        scratch_shapes=[pltpu.SemaphoreType.DMA],
        compiler_params=pltpu.CompilerParams(vmem_limit_bytes=50 << 20),
        cost_estimate=pl.CostEstimate(flops=200_000, bytes_accessed=1 << 20, transcendentals=0),
        name="near",
    )(w, a)


def last_kernel(near, w, *refs):
    total = refs[0][...]
    for a in refs[1:-1]:
        total += a[...]
    refs[-1][...] = near[...] + w[...] * total


def weigh_last(near, w, *arrived):
    return pl.pallas_call(
        last_kernel,
        out_shape=jax.ShapeDtypeStruct(w.shape, f32),
        in_specs=vmem_specs(2 + len(arrived)),
        out_specs=vmem_specs(1)[0],
        compiler_params=pltpu.CompilerParams(vmem_limit_bytes=4 << 20),
        cost_estimate=pl.CostEstimate(flops=300_000, bytes_accessed=1 << 20, transcendentals=0),
        name="last",
    )(near, w, *arrived)


def body(leaves, prod_child, block_weight, block_child, block_parent, block_count, upper_flow):
    prod_child = prod_child.T
    slots = jnp.concatenate([block_child, block_parent])
    nodes = lax.axis_size("nodes")
    batch = lax.axis_size("batch")
    chips, depth = nodes // CORES, batch // ROWS
    ng = leaves.shape[0] * nodes
    pg = prod_child.shape[1]
    qd = upper_flow.shape[0]
    keep = block_weight.shape[0] // batch
    far = depth // 2

    def move(a, dx=0, dc=0):
        to = lambda n: ((n // CORES + dx) % chips) * CORES + (n % CORES + dc) % CORES
        return lax.ppermute(a, "nodes", [(n, to(n)) for n in range(nodes)])

    def shift(a, dz):
        to = lambda b: ((b // ROWS + dz) % depth) * ROWS + b % ROWS
        return lax.ppermute(a, "batch", [(b, to(b)) for b in range(batch)])

    def swap(a, mask):
        return lax.ppermute(a, "batch", [(b, b ^ mask) for b in range(batch)])

    def shift_by_core(a, dz):
        pairs = []
        for n in range(nodes):
            for b in range(batch):
                z = (b // ROWS + (dz if n % CORES == 0 else -dz)) % depth
                pairs.append((n * batch + b, n * batch + z * ROWS + b % ROWS))
        return lax.ppermute(a, ("nodes", "batch"), pairs)

    def gather(a):
        out = []
        for dx in range(chips):
            got = move(a, dx) if dx else a
            out += [got, move(got, 0, 1)]
        return out

    got = gather(leaves)
    one = swap(leaves, 1)
    pair = pack([leaves, one])
    two = swap(pair, 3)
    packed = pack([one, two])
    pieces = gather(packed)

    w, bias = fold(slots, block_count, block_weight, pg, qd)
    sum_values, fx, e, r, pk = forward(prod_child, [pair] + got[1:], w, bias, upper_flow, ng)
    fxs = [fx] + [swap(fx, t) for t in (1, 3, 2)]
    *mine, give = backward(prod_child, w, fx, r, e, nodes, ng)
    given = move(give, 0, 1)
    k = leaves.shape[0]
    flows = [a + given[dx * k : (dx + 1) * k] for dx, a in enumerate(mine)]
    ehl, pks = spread(prod_child, e, pk, pieces, hops(nodes), nodes, flows[1])

    def part(token, *plan):
        return edges(slots, block_count, ehl, pks, bias, fxs, token, plan, keep)

    (e4,) = part(pks, (far,))
    r4 = shift_by_core(e4, 2)
    e3p, e3m = part(e4, (3,), (-3,))
    r3p, r3m = shift(e3p, 1), shift(e3m, -1)
    e1p, e1m, e0 = part(e3m, (1,), (-1,), (0,))
    r1p, r1m = shift(e1p, 1), shift(e1m, -1)
    e2p, e2m = part(e1m, (2,), (-2,))
    c2p, c2m = join(e2p, e2m, r3p, r3m, r4)
    r2p, r2m = shift(c2p, 2), shift(c2m, -2)
    leaf_flow = functools.reduce(
        jnp.add, [flows[0]] + [move(flows[dx], dx) for dx in range(1, chips)]
    )
    near, own = weigh_near(block_weight, e0)
    param_flow = weigh_last(near, own, r1p, r1m, r2p, r2m)
    return sum_values, leaf_flow, param_flow


def solution(mesh):
    placed = (
        P("nodes", None, "batch"),
        P(),
        P("nodes", None, None),
        P("nodes", None),
        P("nodes", None),
        P("nodes"),
        P("nodes", None, "batch"),
    )
    return jax.shard_map(
        body,
        mesh=mesh,
        in_specs=placed,
        out_specs=(
            P("nodes", None, "batch"),
            P("nodes", None, "batch"),
            P(("nodes", "batch"), None, None),
        ),
        check_vma=False,
    )
```

```python
import functools

import jax
import jax.numpy as jnp
from jax import lax
from jax.experimental import pallas as pl
from jax.experimental.pallas import tpu as pltpu
from jax.sharding import PartitionSpec as P


very_low = -1e30
f32, bf16 = jnp.float32, jnp.bfloat16
CORES = 2
ROWS = 4
VMEM = pltpu.VMEM
SMEM = pltpu.SMEM


def parts(x):
    hi = x.astype(bf16)
    lo = (x - hi.astype(f32)).astype(bf16)
    return hi, lo


def quadrants(x):
    g = x.shape[0] // 2
    return (x[:g, :g] + x[:g, g:]) + (x[g:, :g] + x[g:, g:])


def node_at(dx, dc, nodes):
    me = lax.axis_index("nodes")
    x, core = me // CORES, me % CORES
    chips = nodes // CORES
    return ((x + dx) % chips) * CORES + (core + dc) % CORES


def hops(nodes):
    return [(dx, dc) for dx in range(nodes // CORES) for dc in range(CORES)]


def vmem_specs(n):
    return [pl.BlockSpec(memory_space=VMEM)] * n


def fold_kernel(each, count, slots_any, w_hbm, acc, bias, w, slots, sems, sem):
    pg = acc.shape[1]
    steps = w.shape[0] // each
    index = pltpu.make_async_copy(slots_any, slots, sem)
    index.start()
    copies = []
    for j in range(steps):
        at = pl.ds(j * each, each)
        copies.append(pltpu.make_async_copy(w_hbm.at[at], w.at[at], sems.at[j]))
        copies[j].start()

    bias[...] = jnp.full(bias.shape, very_low, f32)

    def clear(c, carry):
        for q in range(acc.shape[0]):
            acc[q, c] = jnp.zeros(acc.shape[2:], f32)
        return carry

    lax.fori_loop(0, pg, clear, 0)
    index.wait()
    for j in range(steps):
        copies[j].wait()

        def add(t, carry, j=j):
            b = j * each + t
            c, q = slots[0, b], slots[1, b]
            live = b < count[0]
            acc[q, c] += w[b] * live.astype(f32)
            row = pl.ds(q * pg + c, 1)
            bias[row, :] = jnp.where(live, 0.0, bias[row, :])
            return carry

        lax.fori_loop(0, each, add, 0, unroll=4)


def fold(slots, block_count, block_weight, pg, qd):
    blocks, g, _ = block_weight.shape
    each = 16
    return pl.pallas_call(
        functools.partial(fold_kernel, each),
        out_shape=(
            jax.ShapeDtypeStruct((qd, pg, g, g), f32),
            jax.ShapeDtypeStruct((qd * pg, g), f32),
        ),
        in_specs=[
            pl.BlockSpec(memory_space=SMEM),
            pl.BlockSpec(memory_space=pl.ANY),
            pl.BlockSpec(memory_space=pltpu.HBM),
        ],
        out_specs=tuple(vmem_specs(2)),
        scratch_shapes=[
            VMEM((blocks, g, g), f32),
            SMEM(slots.shape, jnp.int32),
            pltpu.SemaphoreType.DMA((blocks // each,)),
            pltpu.SemaphoreType.DMA,
        ],
        compiler_params=pltpu.CompilerParams(vmem_limit_bytes=46 << 20),
        cost_estimate=pl.CostEstimate(flops=20_000_000, bytes_accessed=16 << 20, transcendentals=0),
        name="fold",
    )(block_count, slots, block_weight)


def forward_kernel(nodes, prod_child, *refs):
    n = nodes
    got = refs[:n]
    w_ref, bias, up, sv_hbm, fx, e_ref, r_ref, pk, lv, whl, shl, sv, sems = refs[n:]
    pg, g, s = e_ref.shape
    qd = up.shape[0]
    each = lv.shape[0] // n
    for k, (dx, dc) in enumerate(hops(n)):
        src = node_at(-dx, -dc, n)
        lv[pl.ds(src * each, each)] = got[k][0:each]

    def product(p, carry):
        x = lv[prod_child[0, p]] + lv[prod_child[1, p]]
        m = jnp.max(x, axis=0, keepdims=True)
        pk[pl.ds(p, 1), :] = m
        e_ref[p] = jnp.exp(x - m)
        return carry

    lax.fori_loop(0, pg, product, 0, unroll=2)
    tops = []
    for q in range(qd):
        here = slice(q * pg, (q + 1) * pg)
        biased = pk[...] + bias[here]
        top = jnp.max(biased, axis=0, keepdims=True)
        r_ref[here] = jnp.exp(biased - top)
        tops.append(top)

    def scaled(q):
        for c in range(pg):
            at = slice(c * g, (c + 1) * g)
            hi, lo = parts(w_ref[q, c])
            whl[q % 2, 0:g, at] = hi
            whl[q % 2, g : 2 * g, at] = lo
            k = q * pg + c
            hi, lo = parts(e_ref[c] * r_ref[k : k + 1, :])
            shl[q % 2, at, 0:s] = hi
            shl[q % 2, at, s : 2 * s] = lo

    scaled(0)
    copies = []
    for q in range(qd):
        total = quadrants(jnp.dot(whl[q % 2], shl[q % 2], preferred_element_type=f32))
        if q + 1 < qd:
            scaled(q + 1)
        sv[q] = tops[q] + jnp.log(total)
        fx[q] = up[q] / total
        copies.append(pltpu.make_async_copy(sv.at[q], sv_hbm.at[q], sems.at[q]))
        if q > 0:
            copies[q - 1].start()
    copies[-1].start()
    for copy in copies:
        copy.wait()


def forward(prod_child, got, w, bias, up, ng):
    nodes = len(got)
    qd, g, s = up.shape
    pg = prod_child.shape[1]
    return pl.pallas_call(
        functools.partial(forward_kernel, nodes),
        out_shape=(
            jax.ShapeDtypeStruct((qd, g, s), f32),
            jax.ShapeDtypeStruct((qd, g, s), f32),
            jax.ShapeDtypeStruct((pg, g, s), f32),
            jax.ShapeDtypeStruct((qd * pg, s), f32),
            jax.ShapeDtypeStruct((pg, s), f32),
        ),
        in_specs=[pl.BlockSpec(memory_space=SMEM)] + vmem_specs(nodes + 3),
        out_specs=(pl.BlockSpec(memory_space=pltpu.HBM), *vmem_specs(4)),
        scratch_shapes=[
            VMEM((ng, g, s), f32),
            VMEM((2, 2 * g, pg * g), bf16),
            VMEM((2, pg * g, 2 * s), bf16),
            VMEM((qd, g, s), f32),
            pltpu.SemaphoreType.DMA((qd,)),
        ],
        compiler_params=pltpu.CompilerParams(vmem_limit_bytes=20 << 20),
        cost_estimate=pl.CostEstimate(
            flops=2 * qd * 4 * g * s * pg * g, bytes_accessed=8 << 20, transcendentals=pg * g * s
        ),
        name="forward",
    )(prod_child, *got, w, bias, up)


def backward_kernel(nodes, each, prod_child, w_ref, fx, r_ref, e_ref, *refs):
    chips = nodes // CORES
    keep, give, (lf, thl, ghl) = refs[:chips], refs[chips], refs[chips + 1 :]
    qd = fx.shape[0]
    pg, g, s = e_ref.shape
    lf[...] = jnp.zeros(lf.shape, f32)

    def some(step, carry):
        for t in range(each):
            c = step * each + t
            for q in range(qd):
                at = slice(q * g, (q + 1) * g)
                hi, lo = parts(w_ref[q, c].T)
                thl[t, 0:g, at] = hi
                thl[t, g : 2 * g, at] = lo
                hi, lo = parts(fx[q] * r_ref[pl.ds(q * pg + c, 1), :])
                ghl[t, at, 0:s] = hi
                ghl[t, at, s : 2 * s] = lo
        for t in range(each):
            c = step * each + t
            back = quadrants(jnp.dot(thl[t], ghl[t], preferred_element_type=f32))
            flow = back * e_ref[c]
            lf[prod_child[0, c]] += flow
            lf[prod_child[1, c]] += flow
        return carry

    lax.fori_loop(0, pg // each, some, 0)
    for dx in range(chips):
        k = keep[0].shape[0]
        keep[dx][...] = lf[pl.ds(node_at(dx, 0, nodes) * k, k)]
        give[dx * k : (dx + 1) * k] = lf[pl.ds(node_at(dx, 1, nodes) * k, k)]


def backward(prod_child, w, fx, r, e, nodes, ng):
    pg, g, s = e.shape
    qd = fx.shape[0]
    chips = nodes // CORES
    each = 4
    k = ng // nodes
    return pl.pallas_call(
        functools.partial(backward_kernel, nodes, each),
        out_shape=[jax.ShapeDtypeStruct((k, g, s), f32)] * chips
        + [jax.ShapeDtypeStruct((k * chips, g, s), f32)],
        in_specs=[pl.BlockSpec(memory_space=SMEM)] + vmem_specs(4),
        out_specs=vmem_specs(chips + 1),
        scratch_shapes=[
            VMEM((ng, g, s), f32),
            VMEM((each, 2 * g, qd * g), bf16),
            VMEM((each, qd * g, 2 * s), bf16),
        ],
        compiler_params=pltpu.CompilerParams(vmem_limit_bytes=20 << 20),
        cost_estimate=pl.CostEstimate(
            flops=2 * qd * 4 * g * s * pg * g, bytes_accessed=8 << 20, transcendentals=0
        ),
        name="backward",
    )(prod_child, w, fx, r, e)


def pack_kernel(*refs):
    at = 0
    for a in refs[:-1]:
        k = a.shape[0]
        refs[-1][at : at + k] = a[...]
        at += k


def pack(arrays):
    n = sum(a.shape[0] for a in arrays)
    return pl.pallas_call(
        pack_kernel,
        out_shape=jax.ShapeDtypeStruct((n,) + arrays[0].shape[1:], f32),
        in_specs=vmem_specs(len(arrays)),
        out_specs=vmem_specs(1)[0],
        compiler_params=pltpu.CompilerParams(vmem_limit_bytes=4 << 20),
        cost_estimate=pl.CostEstimate(flops=0, bytes_accessed=1 << 20, transcendentals=0),
        name="pack",
    )(*arrays)


def spread_kernel(offsets, prod_child, token, e_own, pk_own, *refs):
    pieces, (ehl, pk) = refs[: len(offsets)], refs[len(offsets) : -1]
    lv = refs[-1]
    pg, g, s = e_own.shape
    sets = lv.shape[0]
    each = pieces[0].shape[0] // sets
    nodes = lv.shape[1] // each
    for (dx, dc), piece in zip(offsets, pieces):
        src = node_at(-dx, -dc, nodes)
        for t in range(sets):
            lv[t, pl.ds(src * each, each)] = piece[t * each : (t + 1) * each]

    def product(p, carry):
        hi, lo = parts(e_own[p])
        ehl[p, 0:g, 0:s] = hi
        ehl[p, g : 2 * g, 0:s] = lo
        pk[0, pl.ds(p, 1), :] = pk_own[pl.ds(p, 1), :]
        a, b = prod_child[0, p], prod_child[1, p]
        for t in range(sets):
            x = lv[t, a] + lv[t, b]
            m = jnp.max(x, axis=0, keepdims=True)
            at = slice((t + 1) * s, (t + 2) * s)
            pk[t + 1, pl.ds(p, 1), :] = m
            hi, lo = parts(jnp.exp(x - m))
            ehl[p, 0:g, at] = hi
            ehl[p, g : 2 * g, at] = lo
        return carry

    lax.fori_loop(0, pg, product, 0, unroll=2)


def spread(prod_child, e, pk, pieces, offsets, nodes, token):
    pg, g, s = e.shape
    sets = ROWS - 1
    each = pieces[0].shape[0] // sets

    def kernel(*refs):
        spread_kernel(offsets, *refs)

    return pl.pallas_call(
        kernel,
        out_shape=(
            jax.ShapeDtypeStruct((pg, 2 * g, (sets + 1) * s), bf16),
            jax.ShapeDtypeStruct((sets + 1, pg, s), f32),
        ),
        in_specs=[pl.BlockSpec(memory_space=SMEM), pl.BlockSpec(memory_space=pl.ANY)]
        + vmem_specs(2 + len(pieces)),
        out_specs=tuple(vmem_specs(2)),
        scratch_shapes=[VMEM((sets, nodes * each, g, s), f32)],
        compiler_params=pltpu.CompilerParams(vmem_limit_bytes=20 << 20),
        cost_estimate=pl.CostEstimate(
            flops=10_000_000, bytes_accessed=10 << 20, transcendentals=pg * g * s * sets
        ),
        name="spread",
    )(prod_child, token, e, pk, *pieces)


def edges_kernel(plan, slots, count, ehl, pk, bias, *refs):
    rows = ROWS
    fxs, refs = refs[:rows], refs[rows:]
    outs, (r, lhs) = refs[1:-2], refs[-2:]
    qd, s = fxs[0].shape[0], fxs[0].shape[2]
    g = fxs[0].shape[1]
    pg = pk.shape[1]
    batch = lax.axis_index("batch")
    z, y = batch // ROWS, batch % ROWS
    depth = lax.axis_size("batch") // ROWS
    for q in range(qd):
        for t in range(rows):
            here = slice(q * pg, (q + 1) * pg)
            biased = pk[t] + bias[here, :]
            r[t, here, :] = jnp.exp(biased - jnp.max(biased, axis=0, keepdims=True))
    for ds, out in zip(plan, outs):
        keep = out.shape[0] // len(ds)
        places = []
        for d in ds:
            first = ((z + d + depth) % depth * ROWS + y) * keep
            places += [first + k for k in range(keep)]
        for k, b in enumerate(places):
            c, q = slots[0, b], slots[1, b]
            live = (b < count[0]).astype(f32)
            for t in range(rows):
                at = slice(t * s, (t + 1) * s)
                hi, lo = parts(fxs[t][q] * (r[t, pl.ds(q * pg + c, 1), :] * live))
                lhs[k, 0:g, at] = hi
                lhs[k, g : 2 * g, at] = lo
        for k, b in enumerate(places):
            c = slots[0, b]
            out[k] = quadrants(
                lax.dot_general(
                    lhs[k], ehl[c], (((1,), (1,)), ((), ())), preferred_element_type=f32
                )
            )


def edges(slots, count, ehl, pk, bias, fxs, token, plan, keep):
    g = ehl.shape[1] // 2
    pg, width = pk.shape[1], ehl.shape[2]
    qd = fxs[0].shape[0]
    counts = [keep * len(ds) for ds in plan]

    def kernel(*refs):
        edges_kernel(plan, *refs)

    return pl.pallas_call(
        kernel,
        out_shape=[jax.ShapeDtypeStruct((n, g, g), f32) for n in counts],
        in_specs=[pl.BlockSpec(memory_space=SMEM)] * 2
        + vmem_specs(3 + len(fxs))
        + [pl.BlockSpec(memory_space=pl.ANY)],
        out_specs=vmem_specs(len(plan)),
        scratch_shapes=[
            VMEM((len(fxs), qd * pg, width // len(fxs)), f32),
            VMEM((max(counts), 2 * g, width), bf16),
        ],
        compiler_params=pltpu.CompilerParams(vmem_limit_bytes=20 << 20),
        cost_estimate=pl.CostEstimate(
            flops=2 * sum(counts) * 4 * g * g * width, bytes_accessed=6 << 20, transcendentals=0
        ),
        name="edges",
    )(slots, count, ehl, pk, bias, *fxs, token)


def join_kernel(ap, am, bp, bm, c_ref, outp, outm):
    first = (lax.axis_index("nodes") % CORES == 0).astype(f32)
    outp[...] = (ap[...] + bp[...]) + c_ref[...] * first
    outm[...] = (am[...] + bm[...]) + c_ref[...] * (1.0 - first)


def join(ap, am, bp, bm, c):
    return pl.pallas_call(
        join_kernel,
        out_shape=[jax.ShapeDtypeStruct(ap.shape, f32)] * 2,
        in_specs=vmem_specs(5),
        out_specs=vmem_specs(2),
        compiler_params=pltpu.CompilerParams(vmem_limit_bytes=4 << 20),
        cost_estimate=pl.CostEstimate(flops=400_000, bytes_accessed=2 << 20, transcendentals=0),
        name="join",
    )(ap, am, bp, bm, c)


def near_kernel(w_hbm, a_ref, near, w, sem):
    keep = w.shape[0]
    own = w_hbm.at[pl.ds(lax.axis_index("batch") * keep, keep)]
    copy = pltpu.make_async_copy(own, w, sem)
    copy.start()
    copy.wait()
    near[...] = w[...] * a_ref[...]


def weigh_near(w, a):
    return pl.pallas_call(
        near_kernel,
        out_shape=[jax.ShapeDtypeStruct(a.shape, f32)] * 2,
        in_specs=[pl.BlockSpec(memory_space=pltpu.HBM)] + vmem_specs(1),
        out_specs=vmem_specs(2),
        scratch_shapes=[pltpu.SemaphoreType.DMA],
        compiler_params=pltpu.CompilerParams(vmem_limit_bytes=50 << 20),
        cost_estimate=pl.CostEstimate(flops=200_000, bytes_accessed=1 << 20, transcendentals=0),
        name="near",
    )(w, a)


def last_kernel(near, w, *refs):
    total = refs[0][...]
    for a in refs[1:-1]:
        total += a[...]
    refs[-1][...] = near[...] + w[...] * total


def weigh_last(near, w, *arrived):
    return pl.pallas_call(
        last_kernel,
        out_shape=jax.ShapeDtypeStruct(w.shape, f32),
        in_specs=vmem_specs(2 + len(arrived)),
        out_specs=vmem_specs(1)[0],
        compiler_params=pltpu.CompilerParams(vmem_limit_bytes=4 << 20),
        cost_estimate=pl.CostEstimate(flops=300_000, bytes_accessed=1 << 20, transcendentals=0),
        name="last",
    )(near, w, *arrived)


def body(leaves, prod_child, block_weight, block_child, block_parent, block_count, upper_flow):
    prod_child = prod_child.T
    slots = jnp.concatenate([block_child, block_parent])
    nodes = lax.axis_size("nodes")
    batch = lax.axis_size("batch")
    chips, depth = nodes // CORES, batch // ROWS
    ng = leaves.shape[0] * nodes
    pg = prod_child.shape[1]
    qd = upper_flow.shape[0]
    keep = block_weight.shape[0] // batch
    far = depth // 2

    def move(a, dx=0, dc=0):
        to = lambda n: ((n // CORES + dx) % chips) * CORES + (n % CORES + dc) % CORES
        return lax.ppermute(a, "nodes", [(n, to(n)) for n in range(nodes)])

    def shift(a, dz):
        to = lambda b: ((b // ROWS + dz) % depth) * ROWS + b % ROWS
        return lax.ppermute(a, "batch", [(b, to(b)) for b in range(batch)])

    def swap(a, mask):
        return lax.ppermute(a, "batch", [(b, b ^ mask) for b in range(batch)])

    def shift_by_core(a, dz):
        pairs = []
        for n in range(nodes):
            for b in range(batch):
                z = (b // ROWS + (dz if n % CORES == 0 else -dz)) % depth
                pairs.append((n * batch + b, n * batch + z * ROWS + b % ROWS))
        return lax.ppermute(a, ("nodes", "batch"), pairs)

    def gather(a):
        out = []
        for dx in range(chips):
            got = move(a, dx) if dx else a
            out += [got, move(got, 0, 1)]
        return out

    got = gather(leaves)
    one = swap(leaves, 1)
    pair = pack([leaves, one])
    two = swap(pair, 3)
    packed = pack([one, two])
    pieces = gather(packed)

    w, bias = fold(slots, block_count, block_weight, pg, qd)
    sum_values, fx, e, r, pk = forward(prod_child, [pair] + got[1:], w, bias, upper_flow, ng)
    fxs = [fx] + [swap(fx, t) for t in (1, 3, 2)]
    *mine, give = backward(prod_child, w, fx, r, e, nodes, ng)
    given = move(give, 0, 1)
    k = leaves.shape[0]
    flows = [a + given[dx * k : (dx + 1) * k] for dx, a in enumerate(mine)]
    ehl, pks = spread(prod_child, e, pk, pieces, hops(nodes), nodes, flows[1])

    def part(token, *plan):
        return edges(slots, block_count, ehl, pks, bias, fxs, token, plan, keep)

    (e3p,) = part(pks, (3,))
    r3p = shift(e3p, 1)
    (e3m,) = part(e3p, (-3,))
    r3m = shift(e3m, -1)
    (e4,) = part(e3m, (far,))
    r4 = shift_by_core(e4, 2)
    e1p, e1m, e0 = part(e4, (1,), (-1,), (0,))
    r1p, r1m = shift(e1p, 1), shift(e1m, -1)
    e2p, e2m = part(e1m, (2,), (-2,))
    c2p, c2m = join(e2p, e2m, r3p, r3m, r4)
    r2p, r2m = shift(c2p, 2), shift(c2m, -2)
    leaf_flow = functools.reduce(
        jnp.add, [flows[0]] + [move(flows[dx], dx) for dx in range(1, chips)]
    )
    near, own = weigh_near(block_weight, e0)
    param_flow = weigh_last(near, own, r1p, r1m, r2p, r2m)
    return sum_values, leaf_flow, param_flow


def solution(mesh):
    placed = (
        P("nodes", None, "batch"),
        P(),
        P("nodes", None, None),
        P("nodes", None),
        P("nodes", None),
        P("nodes"),
        P("nodes", None, "batch"),
    )
    return jax.shard_map(
        body,
        mesh=mesh,
        in_specs=placed,
        out_specs=(
            P("nodes", None, "batch"),
            P("nodes", None, "batch"),
            P(("nodes", "batch"), None, None),
        ),
        check_vma=False,
    )
```

```python
import functools

import jax
import jax.numpy as jnp
from jax import lax
from jax.experimental import pallas as pl
from jax.experimental.pallas import tpu as pltpu
from jax.sharding import PartitionSpec as P


very_low = -1e30
f32, bf16 = jnp.float32, jnp.bfloat16
CORES = 2
ROWS = 4
VMEM = pltpu.VMEM
SMEM = pltpu.SMEM


def parts(x):
    hi = x.astype(bf16)
    lo = (x - hi.astype(f32)).astype(bf16)
    return hi, lo


def quadrants(x):
    g = x.shape[0] // 2
    return (x[:g, :g] + x[:g, g:]) + (x[g:, :g] + x[g:, g:])


def node_at(dx, dc, nodes):
    me = lax.axis_index("nodes")
    x, core = me // CORES, me % CORES
    chips = nodes // CORES
    return ((x + dx) % chips) * CORES + (core + dc) % CORES


def hops(nodes):
    return [(dx, dc) for dx in range(nodes // CORES) for dc in range(CORES)]


def vmem_specs(n):
    return [pl.BlockSpec(memory_space=VMEM)] * n


def fold_kernel(each, count, slots_any, w_hbm, acc, bias, w, slots, sems, sem):
    pg = acc.shape[1]
    steps = w.shape[0] // each
    index = pltpu.make_async_copy(slots_any, slots, sem)
    index.start()
    copies = []
    for j in range(steps):
        at = pl.ds(j * each, each)
        copies.append(pltpu.make_async_copy(w_hbm.at[at], w.at[at], sems.at[j]))
        copies[j].start()

    bias[...] = jnp.full(bias.shape, very_low, f32)

    def clear(c, carry):
        for q in range(acc.shape[0]):
            acc[q, c] = jnp.zeros(acc.shape[2:], f32)
        return carry

    lax.fori_loop(0, pg, clear, 0)
    index.wait()
    for j in range(steps):
        copies[j].wait()

        def add(t, carry, j=j):
            b = j * each + t
            c, q = slots[0, b], slots[1, b]
            live = b < count[0]
            acc[q, c] += w[b] * live.astype(f32)
            row = pl.ds(q * pg + c, 1)
            bias[row, :] = jnp.where(live, 0.0, bias[row, :])
            return carry

        lax.fori_loop(0, each, add, 0, unroll=4)


def fold(slots, block_count, block_weight, pg, qd):
    blocks, g, _ = block_weight.shape
    each = 16
    return pl.pallas_call(
        functools.partial(fold_kernel, each),
        out_shape=(
            jax.ShapeDtypeStruct((qd, pg, g, g), f32),
            jax.ShapeDtypeStruct((qd * pg, g), f32),
        ),
        in_specs=[
            pl.BlockSpec(memory_space=SMEM),
            pl.BlockSpec(memory_space=pl.ANY),
            pl.BlockSpec(memory_space=pltpu.HBM),
        ],
        out_specs=tuple(vmem_specs(2)),
        scratch_shapes=[
            VMEM((blocks, g, g), f32),
            SMEM(slots.shape, jnp.int32),
            pltpu.SemaphoreType.DMA((blocks // each,)),
            pltpu.SemaphoreType.DMA,
        ],
        compiler_params=pltpu.CompilerParams(vmem_limit_bytes=46 << 20),
        cost_estimate=pl.CostEstimate(flops=20_000_000, bytes_accessed=16 << 20, transcendentals=0),
        name="fold",
    )(block_count, slots, block_weight)


def forward_kernel(nodes, prod_child, *refs):
    n = nodes
    got = refs[:n]
    w_ref, bias, up, sv_hbm, fx, e_ref, r_ref, pk, lv, whl, shl, sv, sems = refs[n:]
    pg, g, s = e_ref.shape
    qd = up.shape[0]
    each = lv.shape[0] // n
    for k, (dx, dc) in enumerate(hops(n)):
        src = node_at(-dx, -dc, n)
        lv[pl.ds(src * each, each)] = got[k][0:each]

    def product(p, carry):
        x = lv[prod_child[0, p]] + lv[prod_child[1, p]]
        m = jnp.max(x, axis=0, keepdims=True)
        pk[pl.ds(p, 1), :] = m
        e_ref[p] = jnp.exp(x - m)
        return carry

    lax.fori_loop(0, pg, product, 0, unroll=2)
    tops = []
    for q in range(qd):
        here = slice(q * pg, (q + 1) * pg)
        biased = pk[...] + bias[here]
        top = jnp.max(biased, axis=0, keepdims=True)
        r_ref[here] = jnp.exp(biased - top)
        tops.append(top)

    def scaled(q):
        for c in range(pg):
            at = slice(c * g, (c + 1) * g)
            hi, lo = parts(w_ref[q, c])
            whl[q % 2, 0:g, at] = hi
            whl[q % 2, g : 2 * g, at] = lo
            k = q * pg + c
            hi, lo = parts(e_ref[c] * r_ref[k : k + 1, :])
            shl[q % 2, at, 0:s] = hi
            shl[q % 2, at, s : 2 * s] = lo

    scaled(0)
    copies = []
    for q in range(qd):
        total = quadrants(jnp.dot(whl[q % 2], shl[q % 2], preferred_element_type=f32))
        if q + 1 < qd:
            scaled(q + 1)
        sv[q] = tops[q] + jnp.log(total)
        fx[q] = up[q] / total
        copies.append(pltpu.make_async_copy(sv.at[q], sv_hbm.at[q], sems.at[q]))
        if q > 0:
            copies[q - 1].start()
    copies[-1].start()
    for copy in copies:
        copy.wait()


def forward(prod_child, got, w, bias, up, ng):
    nodes = len(got)
    qd, g, s = up.shape
    pg = prod_child.shape[1]
    return pl.pallas_call(
        functools.partial(forward_kernel, nodes),
        out_shape=(
            jax.ShapeDtypeStruct((qd, g, s), f32),
            jax.ShapeDtypeStruct((qd, g, s), f32),
            jax.ShapeDtypeStruct((pg, g, s), f32),
            jax.ShapeDtypeStruct((qd * pg, s), f32),
            jax.ShapeDtypeStruct((pg, s), f32),
        ),
        in_specs=[pl.BlockSpec(memory_space=SMEM)] + vmem_specs(nodes + 3),
        out_specs=(pl.BlockSpec(memory_space=pltpu.HBM), *vmem_specs(4)),
        scratch_shapes=[
            VMEM((ng, g, s), f32),
            VMEM((2, 2 * g, pg * g), bf16),
            VMEM((2, pg * g, 2 * s), bf16),
            VMEM((qd, g, s), f32),
            pltpu.SemaphoreType.DMA((qd,)),
        ],
        compiler_params=pltpu.CompilerParams(vmem_limit_bytes=20 << 20),
        cost_estimate=pl.CostEstimate(
            flops=2 * qd * 4 * g * s * pg * g, bytes_accessed=8 << 20, transcendentals=pg * g * s
        ),
        name="forward",
    )(prod_child, *got, w, bias, up)


def backward_kernel(nodes, each, prod_child, w_ref, fx, r_ref, e_ref, *refs):
    chips = nodes // CORES
    keep, give, (lf, thl, ghl) = refs[:chips], refs[chips], refs[chips + 1 :]
    qd = fx.shape[0]
    pg, g, s = e_ref.shape
    lf[...] = jnp.zeros(lf.shape, f32)

    def some(step, carry):
        for t in range(each):
            c = step * each + t
            for q in range(qd):
                at = slice(q * g, (q + 1) * g)
                hi, lo = parts(w_ref[q, c].T)
                thl[t, 0:g, at] = hi
                thl[t, g : 2 * g, at] = lo
                hi, lo = parts(fx[q] * r_ref[pl.ds(q * pg + c, 1), :])
                ghl[t, at, 0:s] = hi
                ghl[t, at, s : 2 * s] = lo
        for t in range(each):
            c = step * each + t
            back = quadrants(jnp.dot(thl[t], ghl[t], preferred_element_type=f32))
            flow = back * e_ref[c]
            lf[prod_child[0, c]] += flow
            lf[prod_child[1, c]] += flow
        return carry

    lax.fori_loop(0, pg // each, some, 0)
    for dx in range(chips):
        k = keep[0].shape[0]
        keep[dx][...] = lf[pl.ds(node_at(dx, 0, nodes) * k, k)]
        give[dx * k : (dx + 1) * k] = lf[pl.ds(node_at(dx, 1, nodes) * k, k)]


def backward(prod_child, w, fx, r, e, nodes, ng):
    pg, g, s = e.shape
    qd = fx.shape[0]
    chips = nodes // CORES
    each = 4
    k = ng // nodes
    return pl.pallas_call(
        functools.partial(backward_kernel, nodes, each),
        out_shape=[jax.ShapeDtypeStruct((k, g, s), f32)] * chips
        + [jax.ShapeDtypeStruct((k * chips, g, s), f32)],
        in_specs=[pl.BlockSpec(memory_space=SMEM)] + vmem_specs(4),
        out_specs=vmem_specs(chips + 1),
        scratch_shapes=[
            VMEM((ng, g, s), f32),
            VMEM((each, 2 * g, qd * g), bf16),
            VMEM((each, qd * g, 2 * s), bf16),
        ],
        compiler_params=pltpu.CompilerParams(vmem_limit_bytes=20 << 20),
        cost_estimate=pl.CostEstimate(
            flops=2 * qd * 4 * g * s * pg * g, bytes_accessed=8 << 20, transcendentals=0
        ),
        name="backward",
    )(prod_child, w, fx, r, e)


def pack_kernel(*refs):
    at = 0
    for a in refs[:-1]:
        k = a.shape[0]
        refs[-1][at : at + k] = a[...]
        at += k


def pack(arrays):
    n = sum(a.shape[0] for a in arrays)
    return pl.pallas_call(
        pack_kernel,
        out_shape=jax.ShapeDtypeStruct((n,) + arrays[0].shape[1:], f32),
        in_specs=vmem_specs(len(arrays)),
        out_specs=vmem_specs(1)[0],
        compiler_params=pltpu.CompilerParams(vmem_limit_bytes=4 << 20),
        cost_estimate=pl.CostEstimate(flops=0, bytes_accessed=1 << 20, transcendentals=0),
        name="pack",
    )(*arrays)


def spread_kernel(offsets, prod_child, token, e_own, pk_own, *refs):
    pieces, (ehl, pk) = refs[: len(offsets)], refs[len(offsets) : -1]
    lv = refs[-1]
    pg, g, s = e_own.shape
    sets = lv.shape[0]
    each = pieces[0].shape[0] // sets
    nodes = lv.shape[1] // each
    for (dx, dc), piece in zip(offsets, pieces):
        src = node_at(-dx, -dc, nodes)
        for t in range(sets):
            lv[t, pl.ds(src * each, each)] = piece[t * each : (t + 1) * each]

    def product(p, carry):
        hi, lo = parts(e_own[p])
        ehl[p, 0:g, 0:s] = hi
        ehl[p, g : 2 * g, 0:s] = lo
        pk[0, pl.ds(p, 1), :] = pk_own[pl.ds(p, 1), :]
        a, b = prod_child[0, p], prod_child[1, p]
        for t in range(sets):
            x = lv[t, a] + lv[t, b]
            m = jnp.max(x, axis=0, keepdims=True)
            at = slice((t + 1) * s, (t + 2) * s)
            pk[t + 1, pl.ds(p, 1), :] = m
            hi, lo = parts(jnp.exp(x - m))
            ehl[p, 0:g, at] = hi
            ehl[p, g : 2 * g, at] = lo
        return carry

    lax.fori_loop(0, pg, product, 0, unroll=2)


def spread(prod_child, e, pk, pieces, offsets, nodes, token):
    pg, g, s = e.shape
    sets = ROWS - 1
    each = pieces[0].shape[0] // sets

    def kernel(*refs):
        spread_kernel(offsets, *refs)

    return pl.pallas_call(
        kernel,
        out_shape=(
            jax.ShapeDtypeStruct((pg, 2 * g, (sets + 1) * s), bf16),
            jax.ShapeDtypeStruct((sets + 1, pg, s), f32),
        ),
        in_specs=[pl.BlockSpec(memory_space=SMEM), pl.BlockSpec(memory_space=pl.ANY)]
        + vmem_specs(2 + len(pieces)),
        out_specs=tuple(vmem_specs(2)),
        scratch_shapes=[VMEM((sets, nodes * each, g, s), f32)],
        compiler_params=pltpu.CompilerParams(vmem_limit_bytes=20 << 20),
        cost_estimate=pl.CostEstimate(
            flops=10_000_000, bytes_accessed=10 << 20, transcendentals=pg * g * s * sets
        ),
        name="spread",
    )(prod_child, token, e, pk, *pieces)


def edges_kernel(plan, slots, count, ehl, pk, bias, *refs):
    rows = ROWS
    fxs, refs = refs[:rows], refs[rows:]
    outs, (r, lhs) = refs[1:-2], refs[-2:]
    qd, s = fxs[0].shape[0], fxs[0].shape[2]
    g = fxs[0].shape[1]
    pg = pk.shape[1]
    batch = lax.axis_index("batch")
    z, y = batch // ROWS, batch % ROWS
    depth = lax.axis_size("batch") // ROWS
    for q in range(qd):
        for t in range(rows):
            here = slice(q * pg, (q + 1) * pg)
            biased = pk[t] + bias[here, :]
            r[t, here, :] = jnp.exp(biased - jnp.max(biased, axis=0, keepdims=True))
    for ds, out in zip(plan, outs):
        keep = out.shape[0] // len(ds)
        places = []
        for d in ds:
            first = ((z + d + depth) % depth * ROWS + y) * keep
            places += [first + k for k in range(keep)]
        for k, b in enumerate(places):
            c, q = slots[0, b], slots[1, b]
            live = (b < count[0]).astype(f32)
            for t in range(rows):
                at = slice(t * s, (t + 1) * s)
                hi, lo = parts(fxs[t][q] * (r[t, pl.ds(q * pg + c, 1), :] * live))
                lhs[k, 0:g, at] = hi
                lhs[k, g : 2 * g, at] = lo
        for k, b in enumerate(places):
            c = slots[0, b]
            out[k] = quadrants(
                lax.dot_general(
                    lhs[k], ehl[c], (((1,), (1,)), ((), ())), preferred_element_type=f32
                )
            )


def edges(slots, count, ehl, pk, bias, fxs, token, plan, keep):
    g = ehl.shape[1] // 2
    pg, width = pk.shape[1], ehl.shape[2]
    qd = fxs[0].shape[0]
    counts = [keep * len(ds) for ds in plan]

    def kernel(*refs):
        edges_kernel(plan, *refs)

    return pl.pallas_call(
        kernel,
        out_shape=[jax.ShapeDtypeStruct((n, g, g), f32) for n in counts],
        in_specs=[pl.BlockSpec(memory_space=SMEM)] * 2
        + vmem_specs(3 + len(fxs))
        + [pl.BlockSpec(memory_space=pl.ANY)],
        out_specs=vmem_specs(len(plan)),
        scratch_shapes=[
            VMEM((len(fxs), qd * pg, width // len(fxs)), f32),
            VMEM((max(counts), 2 * g, width), bf16),
        ],
        compiler_params=pltpu.CompilerParams(vmem_limit_bytes=20 << 20),
        cost_estimate=pl.CostEstimate(
            flops=2 * sum(counts) * 4 * g * g * width, bytes_accessed=6 << 20, transcendentals=0
        ),
        name="edges",
    )(slots, count, ehl, pk, bias, *fxs, token)


def join_kernel(core, a, b, c, out):
    mine = (lax.axis_index("nodes") % CORES == core).astype(f32)
    out[...] = (a[...] + b[...]) + c[...] * mine


def join(a, b, c, core):
    return pl.pallas_call(
        functools.partial(join_kernel, core),
        out_shape=jax.ShapeDtypeStruct(a.shape, f32),
        in_specs=vmem_specs(3),
        out_specs=vmem_specs(1)[0],
        compiler_params=pltpu.CompilerParams(vmem_limit_bytes=4 << 20),
        cost_estimate=pl.CostEstimate(flops=200_000, bytes_accessed=1 << 20, transcendentals=0),
        name="join",
    )(a, b, c)


def near_kernel(w_hbm, a_ref, near, w, sem):
    keep = w.shape[0]
    own = w_hbm.at[pl.ds(lax.axis_index("batch") * keep, keep)]
    copy = pltpu.make_async_copy(own, w, sem)
    copy.start()
    copy.wait()
    near[...] = w[...] * a_ref[...]


def weigh_near(w, a):
    return pl.pallas_call(
        near_kernel,
        out_shape=[jax.ShapeDtypeStruct(a.shape, f32)] * 2,
        in_specs=[pl.BlockSpec(memory_space=pltpu.HBM)] + vmem_specs(1),
        out_specs=vmem_specs(2),
        scratch_shapes=[pltpu.SemaphoreType.DMA],
        compiler_params=pltpu.CompilerParams(vmem_limit_bytes=50 << 20),
        cost_estimate=pl.CostEstimate(flops=200_000, bytes_accessed=1 << 20, transcendentals=0),
        name="near",
    )(w, a)


def last_kernel(near, w, *refs):
    total = refs[0][...]
    for a in refs[1:-1]:
        total += a[...]
    refs[-1][...] = near[...] + w[...] * total


def weigh_last(near, w, *arrived):
    return pl.pallas_call(
        last_kernel,
        out_shape=jax.ShapeDtypeStruct(w.shape, f32),
        in_specs=vmem_specs(2 + len(arrived)),
        out_specs=vmem_specs(1)[0],
        compiler_params=pltpu.CompilerParams(vmem_limit_bytes=4 << 20),
        cost_estimate=pl.CostEstimate(flops=300_000, bytes_accessed=1 << 20, transcendentals=0),
        name="last",
    )(near, w, *arrived)


def body(leaves, prod_child, block_weight, block_child, block_parent, block_count, upper_flow):
    prod_child = prod_child.T
    slots = jnp.concatenate([block_child, block_parent])
    nodes = lax.axis_size("nodes")
    batch = lax.axis_size("batch")
    chips, depth = nodes // CORES, batch // ROWS
    ng = leaves.shape[0] * nodes
    pg = prod_child.shape[1]
    qd = upper_flow.shape[0]
    keep = block_weight.shape[0] // batch
    far = depth // 2

    def move(a, dx=0, dc=0):
        to = lambda n: ((n // CORES + dx) % chips) * CORES + (n % CORES + dc) % CORES
        return lax.ppermute(a, "nodes", [(n, to(n)) for n in range(nodes)])

    def shift(a, dz):
        to = lambda b: ((b // ROWS + dz) % depth) * ROWS + b % ROWS
        return lax.ppermute(a, "batch", [(b, to(b)) for b in range(batch)])

    def swap(a, mask):
        return lax.ppermute(a, "batch", [(b, b ^ mask) for b in range(batch)])

    def shift_by_core(a, dz):
        pairs = []
        for n in range(nodes):
            for b in range(batch):
                z = (b // ROWS + (dz if n % CORES == 0 else -dz)) % depth
                pairs.append((n * batch + b, n * batch + z * ROWS + b % ROWS))
        return lax.ppermute(a, ("nodes", "batch"), pairs)

    def gather(a):
        out = []
        for dx in range(chips):
            got = move(a, dx) if dx else a
            out += [got, move(got, 0, 1)]
        return out

    got = gather(leaves)
    one = swap(leaves, 1)
    pair = pack([leaves, one])
    two = swap(pair, 3)
    packed = pack([one, two])
    pieces = gather(packed)

    w, bias = fold(slots, block_count, block_weight, pg, qd)
    sum_values, fx, e, r, pk = forward(prod_child, [pair] + got[1:], w, bias, upper_flow, ng)
    fxs = [fx] + [swap(fx, t) for t in (1, 3, 2)]
    *mine, give = backward(prod_child, w, fx, r, e, nodes, ng)
    given = move(give, 0, 1)
    k = leaves.shape[0]
    flows = [a + given[dx * k : (dx + 1) * k] for dx, a in enumerate(mine)]
    ehl, pks = spread(prod_child, e, pk, pieces, hops(nodes), nodes, flows[1])

    def part(token, *plan):
        return edges(slots, block_count, ehl, pks, bias, fxs, token, plan, keep)

    (e4,) = part(pks, (far,))
    r4 = shift_by_core(e4, 2)
    e3p, e3m = part(e4, (3,), (-3,))
    r3p, r3m = shift(e3p, 1), shift(e3m, -1)
    e1p, e1m, e0 = part(e3m, (1,), (-1,), (0,))
    r1p, r1m = shift(e1p, 1), shift(e1m, -1)
    e2p, e2m = part(e1m, (2,), (-2,))
    c2m = join(e2m, r3m, r4, 1)
    r2m = shift(c2m, -2)
    c2p = join(e2p, r3p, r4, 0)
    r2p = shift(c2p, 2)
    leaf_flow = functools.reduce(
        jnp.add, [flows[0]] + [move(flows[dx], dx) for dx in range(1, chips)]
    )
    near, own = weigh_near(block_weight, e0)
    param_flow = weigh_last(near, own, r1p, r1m, r2p, r2m)
    return sum_values, leaf_flow, param_flow


def solution(mesh):
    placed = (
        P("nodes", None, "batch"),
        P(),
        P("nodes", None, None),
        P("nodes", None),
        P("nodes", None),
        P("nodes"),
        P("nodes", None, "batch"),
    )
    return jax.shard_map(
        body,
        mesh=mesh,
        in_specs=placed,
        out_specs=(
            P("nodes", None, "batch"),
            P("nodes", None, "batch"),
            P(("nodes", "batch"), None, None),
        ),
        check_vma=False,
    )
```
